512 devices in a mesh: segment: 4 (over y_lo, core), band: 128 (over z, x, y_hi).
Axes of the slice: x: 4, y: 4 (y_hi: 2, y_lo: 2; y = y_hi * 2 + y_lo), z: 16, core: 2. Of those that a mesh axis runs over, the one named last changes fastest.
Arguments:
- voltages: bfloat16 [2, 2048, 16384], P(None, 'band', 'segment'), may hold values from -6 to 6
- slot_of_antenna: int32 [2048], replicated, may hold values from 0 to 2047, each once
- antenna_positions: int32 [2048, 2], replicated, may hold values from -1000 to 999
- beam_directions: int32 [1024, 2], replicated, may hold values from -64 to 63
Outputs:
- vis_real: float32 [128, 4, 256, 2048], P('band', 'segment')
- vis_imag: float32 [128, 4, 256, 2048], P('band', 'segment')
- beam_series: float32 [2, 4, 128, 2, 16384], P(None, 'segment', 'band')
The draws below stay inside these ranges and needn't reach their ends.
Inputs may be any that keep to these rules, and one draw needn't show every extreme that they name: `slot_of_antenna`: a permutation of the antennas.
All inputs are finite; a program needn't handle non-finite values.
Results may differ from the reference program's by a relative error of at most 0.005.
Values may be sent and summed in bfloat16 or wider, within the bound.
A program may use at most 64 MiB of HBM per device.

```python
import math
import jax
import jax.numpy as jnp
from jax import lax

A = 2048
C = 64
BEAMS = 1024
NB = 256
NS = 16384
ROWBLK = 256
BEAMBLK = 128
N_SEGMENT = 4


def with_ends(array, rng, least, top_value):
    longest = array.shape.index(max(array.shape))
    spots = []
    for shift in (0, 1):
        where = [jax.random.randint(jax.random.fold_in(rng, axis), (), 0, length) for axis, length in enumerate(array.shape)]
        where[longest] = (where[longest] + shift) % array.shape[longest]
        spots.append(tuple(where))
    return array.at[spots[0]].set(least).at[spots[1]].set(top_value)


def block_levels(rng, shape, shards, smallest, top_value):
    level, own = 1.0, jax.random.fold_in(rng, 6)
    for position, blocks in shards:
        draws = jnp.exp(jax.random.uniform(jax.random.fold_in(own, position), (blocks,), jnp.float32, smallest / len(shards), top_value / len(shards)))
        level = level * jnp.repeat(draws, shape[position] // blocks).reshape([-1 if axis == position else 1 for axis in range(len(shape))])
    return level


def noise(rng, extent, spread, reach, shards=(), kind=jnp.bfloat16):
    values = spread * jax.random.normal(rng, extent, jnp.float32)
    if shards:
        values = values * block_levels(rng, extent, shards, -0.22, 0.18)
    return jnp.clip(values, -reach, reach).astype(kind)


def setup_inputs(seed: int = 0) -> dict:
    arg_keys = jax.random.split(jax.random.key(seed), 5)
    voltages = noise(arg_keys[0], (2, A, NS), 1.0, 6.0, ((1, 128), (2, 4)))
    slot_of_antenna = jax.random.permutation(arg_keys[1], A).astype(jnp.int32)
    antenna_positions = with_ends(jax.random.randint(arg_keys[2], (A, 2), -1000, 1000), jax.random.fold_in(arg_keys[2], 1), -1000, 999).astype(jnp.int32)
    beam_directions = with_ends(jax.random.randint(arg_keys[3], (BEAMS, 2), -64, 64), jax.random.fold_in(arg_keys[3], 1), -64, 63).astype(jnp.int32)
    return {"voltages": voltages, "slot_of_antenna": slot_of_antenna, "antenna_positions": antenna_positions, "beam_directions": beam_directions}


def dft_parts():
    index = jnp.arange(64, dtype=jnp.int32)
    product = jnp.remainder(index[:, None] * index[None, :], 64).astype(jnp.float32)
    theta = product * (2.0 * math.pi / 64.0)
    return (jnp.cos(theta) * 0.125, jnp.sin(theta) * 0.125)

def forward_table():
    cosine, sine = dft_parts()
    return jnp.stack([jnp.stack([cosine, -sine], axis=1), jnp.stack([sine, cosine], axis=1)])

def inverse_table():
    cosine, sine = dft_parts()
    return jnp.stack([jnp.stack([cosine, sine], axis=1), jnp.stack([-sine, cosine], axis=1)])

def channelize(samples):
    count = samples.shape[2] // 64
    values = samples.astype(jnp.float32).reshape(2, samples.shape[1], count, 64)
    spectra = jnp.einsum('pajn,pnqk->kqaj', values, forward_table(), precision=lax.Precision.HIGHEST)
    return spectra.astype(jnp.bfloat16)

def steering(channel, directions, positions):
    delay = jnp.remainder(directions[:, 0:1] * positions[None, :, 0] + directions[:, 1:2] * positions[None, :, 1], 64).astype(jnp.int32)
    phase = jnp.remainder(channel * delay, 64).astype(jnp.float32) * (2.0 * math.pi / 64.0)
    return jnp.stack([jnp.cos(phase), -jnp.sin(phase)]).astype(jnp.bfloat16)

def reference(voltages, slot_of_antenna, antenna_positions, beam_directions):
    spectra = channelize(voltages)
    ordered = spectra[:, :, slot_of_antenna, :]
    inverse_count = 1.0 / NB
    beam_scale = 1.0 / math.sqrt(A)

    def one_channel(item):
        channel, block = item
        data = block.astype(jnp.float32)
        turned = jnp.stack([data[1], -data[0]])
        real_part = jnp.einsum('pat,pbt->ab', data, data, precision=lax.Precision.HIGHEST) * inverse_count
        imag_part = jnp.einsum('pat,pbt->ab', turned, data, precision=lax.Precision.HIGHEST) * inverse_count
        weight = steering(channel, beam_directions, antenna_positions).astype(jnp.float32)
        mixed = jnp.einsum('gba,pat->gbpt', weight, data, precision=lax.Precision.HIGHEST)
        formed_real = mixed[0, :, 0] - mixed[1, :, 1]
        formed_imag = mixed[0, :, 1] + mixed[1, :, 0]
        formed = jnp.stack([formed_real, formed_imag], axis=1) * beam_scale
        return (real_part, imag_part, formed)
    real_all, imag_all, formed_all = lax.map(one_channel, (jnp.arange(C, dtype=jnp.int32), ordered))
    series = jnp.einsum('kbpj,pkqn->bqjn', formed_all, inverse_table(), precision=lax.Precision.HIGHEST)
    series = series.reshape(2, N_SEGMENT, BEAMBLK, 2, NB * 64)
    vis_real = real_all.reshape(2 * C, N_SEGMENT, ROWBLK, A)
    vis_imag = imag_all.reshape(2 * C, N_SEGMENT, ROWBLK, A)
    return (vis_real, vis_imag, series)
```

```python
import functools
import math

import jax
import jax.numpy as jnp
import numpy as np
from jax import lax
from jax.experimental import pallas as pl
from jax.experimental.pallas import tpu as pltpu
from jax.sharding import PartitionSpec as P

A = 2048
C = 64
BEAMS = 1024
NB = 256
MESH = pl.DeviceIdType.MESH


def dft_parts():
    index = np.arange(64)
    theta = (np.outer(index, index) % 64) * (2.0 * math.pi / 64.0)
    return np.cos(theta) * 0.125, np.sin(theta) * 0.125


def split(table):
    high = table.astype(np.float32).astype(jnp.bfloat16)
    low = (table - high.astype(np.float64)).astype(np.float32).astype(jnp.bfloat16)
    return high, low


def forward_tables():
    cosine, sine = dft_parts()
    parts = np.array([[cosine, -sine], [sine, cosine]])
    table = np.zeros((2, 2, 64, 2, 2, 64))
    for t1 in range(2):
        table[:, t1, :, :, t1, :] = parts.transpose(1, 3, 0, 2)
    return split(table.reshape(256, 256))


def inverse_table():
    cosine, sine = dft_parts()
    return np.array([[cosine, sine], [-sine, cosine]]).transpose(0, 2, 1, 3)


def steering_table():
    phase = np.arange(64) * (2.0 * math.pi / 64.0)
    row = np.concatenate([np.cos(phase), -np.sin(phase)]).astype(np.float32)
    return np.broadcast_to(row, (128, 128))


def place():
    segment = lax.axis_index("segment")
    band = lax.axis_index("band")
    core, half, channel = segment % 2, band % 2, band // 2
    return segment, band, core, half, channel, channel // 4, channel % 4, half * 2 + segment // 2


def offset_of(step):
    odd = step % 2
    return (8 + odd * (-(step + 1) // 2) + (1 - odd) * (step // 2)) % 16


def channelize(v_ref, high_ref, low_ref, wide, turned, spectra_f, spectra):
    for p in range(2):
        for t2 in range(32):
            wide[p, t2 * 16 : (t2 + 1) * 16, :] = v_ref[p, :, t2 * 128 : (t2 + 1) * 128].astype(
                jnp.float32
            )
    for a in range(16):
        for p in range(2):
            turned[a * 32 : (a + 1) * 32, p * 128 : (p + 1) * 128] = wide[
                p, pl.ds(a, 32, stride=16), :
            ].astype(jnp.bfloat16)
    dims = (((1,), (1,)), ((), ()))
    lane = lax.broadcasted_iota(jnp.int32, (64, 128), 1)
    first, even = lane < 64, (lane // 32) % 2 == 0
    for g in range(4):
        block = turned[g * 128 : (g + 1) * 128, :]
        out = lax.dot_general(high_ref[...], block, dims, preferred_element_type=jnp.float32)
        out += lax.dot_general(low_ref[...], block, dims, preferred_element_type=jnp.float32)
        part = [out[i * 64 : (i + 1) * 64] for i in range(4)]
        for i in range(2):
            a, b = part[i], part[i + 2]
            part[i] = jnp.where(first, a, pltpu.roll(b, 64, 1))
            part[i + 2] = jnp.where(first, pltpu.roll(a, 64, 1), b)
        for i in (0, 2):
            a, b = part[i], part[i + 1]
            part[i] = jnp.where(even, a, pltpu.roll(b, 32, 1))
            part[i + 1] = jnp.where(even, pltpu.roll(a, 96, 1), b)
        for i in range(4):
            spectra_f[pl.ds(g * 4 + i, 64, stride=16), :] = part[i]
    spectra[...] = spectra_f[...].astype(jnp.bfloat16)


def gather_kernel(
    v_ref, high_ref, low_ref, x_ref,
    wide, turned, spectra_f, spectra,
    send_a, recv_a, own_sem, send_y, recv_y, send_c, recv_c,
):
    segment, band, core, half, channel, z, x, y = place()

    def column(y_to, core_to):
        return ((y_to % 2) * 2 + core_to, channel * 2 + y_to // 2)

    up, down = (y + 1) % 4, (y + 3) % 4
    partner = column(y, 1 - core)
    barrier = pltpu.get_barrier_semaphore()

    def greet(step, carry):
        other = (channel + step) % 64
        pl.semaphore_signal(
            barrier, inc=1, device_id=(segment, other * 2 + half), device_id_type=MESH
        )
        return carry

    lax.fori_loop(1, 64, greet, 0)
    for target in (column(up, core), column(down, core), partner):
        pl.semaphore_signal(barrier, inc=1, device_id=target, device_id_type=MESH)

    channelize(v_ref, high_ref, low_ref, wide, turned, spectra_f, spectra)

    pl.semaphore_wait(barrier, 66)

    def chunk(y_from, core_from, z_from, rows):
        row = pl.multiple_of((y_from // 2) * 1024 + z_from * 64, 64)
        lane = pl.multiple_of(((y_from % 2) * 2 + core_from) * 128, 128)
        return x_ref.at[pl.ds(row, rows), pl.ds(lane, 128)]

    home = x_ref.at[
        pl.ds(pl.multiple_of(half * 1024 + channel * 16, 16), 16),
        pl.ds(pl.multiple_of(segment * 128, 128), 128),
    ]

    def message(step, across):
        to = ((z + offset_of(step)) % 16) * 4 + (x + across) % 4
        return pltpu.make_async_remote_copy(
            src_ref=spectra.at[pl.ds(pl.multiple_of(to * 16, 16), 16), :],
            dst_ref=home,
            send_sem=send_a,
            recv_sem=recv_a.at[step],
            device_id=(segment, to * 2 + half),
            device_id_type=MESH,
        )

    def send(step, carry):
        for across in range(4):
            message(step, across).start()
        return carry

    lax.fori_loop(0, 15, send, 0)
    for across in range(1, 4):
        message(15, across).start()
    own = pltpu.make_async_copy(
        spectra.at[pl.ds(pl.multiple_of(channel * 16, 16), 16), :], home, own_sem
    )
    own.start()

    def forward(y_from, step, target, send_sem, recv_sem):
        source = chunk(y_from, core, (z + 16 - offset_of(step)) % 16, 64)
        return pltpu.make_async_remote_copy(
            src_ref=source,
            dst_ref=source,
            send_sem=send_sem,
            recv_sem=recv_sem,
            device_id=target,
            device_id_type=MESH,
        )

    relay_from = (y + 3 + 2 * core) % 4
    relay_to = (y + 1 + 2 * core) % 4
    across_from = (y + 2) % 4

    def arrived(ref, sem):
        pltpu.make_async_copy(ref, ref, sem).wait()

    def to_partner(y_from, kind, step):
        forward(y_from, step, partner, send_c.at[kind], recv_c.at[kind]).start()

    def level0(step):
        forward(y, step, column(up, core), send_y.at[0], recv_y.at[0, step]).start()
        forward(y, step, column(down, core), send_y.at[1], recv_y.at[1, step]).start()
        to_partner(y, 0, step)

    def level1(step):
        first = forward(down, step, partner, send_y.at[0], recv_y.at[0, step])
        second = forward(up, step, partner, send_y.at[1], recv_y.at[1, step])
        first.wait_recv()
        second.wait_recv()
        forward(relay_from, step, column(relay_to, core), send_y.at[2], recv_y.at[2, step]).start()
        to_partner(down, 1, step)
        to_partner(up, 2, step)

    def level2(step):
        forward(across_from, step, partner, send_y.at[2], recv_y.at[2, step]).wait_recv()
        to_partner(across_from, 3, step)

    def wait_level0(step):
        z_from = (z + 16 - offset_of(step)) % 16
        arrived(chunk(y, core, z_from, 64), recv_a.at[step])

    wait_level0(0)
    level0(0)
    wait_level0(1)
    level0(1)
    level1(0)

    def body(step, carry):
        wait_level0(step)
        level0(step)
        level1(step - 1)
        level2(step - 2)
        return carry

    lax.fori_loop(2, 15, body, 0)
    own.wait()
    arrived(x_ref.at[pl.ds(0, 48), pl.ds(0, 128)], recv_a.at[15])
    level0(15)
    level1(14)
    level2(13)
    level1(15)
    level2(14)
    level2(15)

    def plane(y_from, core_from):
        return chunk(y_from, core_from, 0, 1024)

    for kind, y_from in enumerate((y, down, up, across_from)):
        arrived(plane(y_from, 1 - core), recv_c.at[kind])
        arrived(plane(y_from, core), send_c.at[kind])
    for kind in range(3):
        arrived(plane(y, core), send_y.at[kind])
    arrived(spectra.at[pl.ds(0, 63 * 16), :], send_a)


def column_of(row):
    return jnp.transpose(jnp.broadcast_to(row, (128, 128)))


def local_kernel(
    x_ref, slot_ref, pos_ref, dir_ref, tab_ref, real_ref, imag_ref, formed_ref,
    pick, weight_a, weight_u, ordered, left,
):
    segment, band, core, half, channel, z, x, y = place()

    lane = lax.broadcasted_iota(jnp.int32, (128, 128), 1)
    for r in range(16):
        slot = column_of(slot_ref[r : r + 1, :])
        for c in range(16):
            position = lane + c * 128
            name = ((position % 1024) // 16) * 32 + (position // 1024) * 16 + position % 16
            pick[r * 128 : (r + 1) * 128, c * 128 : (c + 1) * 128] = jnp.where(
                slot == name, 1.0, 0.0
            ).astype(jnp.bfloat16)

    start = pl.multiple_of(half * 512 + segment * 128, 128)
    turn0 = column_of(dir_ref[0:1, pl.ds(start, 128)]) * channel
    turn1 = column_of(dir_ref[1:2, pl.ds(start, 128)]) * channel
    table = tab_ref[...]
    for c in range(16):
        sl = slice(c * 128, (c + 1) * 128)
        phase = (turn0 * pos_ref[0:1, sl] + turn1 * pos_ref[1:2, sl]) & 63
        weight_a[0:128, sl] = jnp.take_along_axis(table, phase, axis=1).astype(jnp.bfloat16)
        weight_a[128:256, sl] = jnp.take_along_axis(table, phase + 64, axis=1).astype(jnp.bfloat16)

    for c in range(8):
        sl = slice(c * 256, (c + 1) * 256)
        weight_u[:, sl] = jnp.dot(
            weight_a[...], pick[:, sl], preferred_element_type=jnp.float32
        ).astype(jnp.bfloat16)

    low_lane = lax.broadcasted_iota(jnp.int32, (128, 128), 1) < 64
    beam_scale = 1.0 / math.sqrt(A)
    mixed = jnp.dot(weight_u[...], x_ref[...], preferred_element_type=jnp.float32)
    for s in range(4):
        sl = slice(s * 128, (s + 1) * 128)
        other = pltpu.roll(mixed[128:256, sl], 64, 1)
        formed = mixed[0:128, sl] + jnp.where(low_lane, -other, other)
        formed_ref[:, sl] = (formed * beam_scale).astype(jnp.bfloat16)

    def reorder(step, carry):
        rows = pl.ds(pl.multiple_of(step * 256, 256), 256)
        ordered[rows, :] = jnp.dot(
            pick[rows, :], x_ref[...], preferred_element_type=jnp.float32
        ).astype(jnp.bfloat16)
        return carry

    lax.fori_loop(0, 8, reorder, 0)

    mine = ordered[pl.ds(pl.multiple_of((half * 4 + segment) * 256, 256), 256), :]
    low_lanes = lax.broadcasted_iota(jnp.int32, (256, 128), 1) < 64
    left[0:256, :] = mine
    for s in range(4):
        sl = slice(s * 128, (s + 1) * 128)
        other = pltpu.roll(mine[:, sl].astype(jnp.float32), 64, 1)
        left[256:512, sl] = jnp.where(low_lanes, other, -other).astype(jnp.bfloat16)
    dims = (((1,), (1,)), ((), ()))
    for b in range(8):
        sl = slice(b * 256, (b + 1) * 256)
        gram = lax.dot_general(left[...], ordered[sl, :], dims, preferred_element_type=jnp.float32)
        gram = gram * (1.0 / NB)
        real_ref[:, sl] = gram[0:256]
        imag_ref[:, sl] = gram[256:512]


VMEM = pl.BlockSpec(memory_space=pltpu.VMEM)


def per_device(voltages, slot_of_antenna, antenna_positions, beam_directions):
    high, low = forward_tables()
    spectra = pl.pallas_call(
        gather_kernel,
        out_shape=jax.ShapeDtypeStruct((A, 512), jnp.bfloat16),
        in_specs=[VMEM] * 3,
        out_specs=VMEM,
        scratch_shapes=[
            pltpu.VMEM((2, 512, 128), jnp.float32),
            pltpu.VMEM((512, 256), jnp.bfloat16),
            pltpu.VMEM((1024, 128), jnp.float32),
            pltpu.VMEM((1024, 128), jnp.bfloat16),
            pltpu.SemaphoreType.DMA,
            pltpu.SemaphoreType.DMA((16,)),
            pltpu.SemaphoreType.DMA,
            pltpu.SemaphoreType.DMA((3,)),
            pltpu.SemaphoreType.DMA((3, 16)),
            pltpu.SemaphoreType.DMA((4,)),
            pltpu.SemaphoreType.DMA((4,)),
        ],
        compiler_params=pltpu.CompilerParams(collective_id=0, has_side_effects=True),
        name="exchange",
    )(voltages, jnp.asarray(high), jnp.asarray(low))
    real, imag, formed = pl.pallas_call(
        local_kernel,
        out_shape=(
            jax.ShapeDtypeStruct((256, A), jnp.float32),
            jax.ShapeDtypeStruct((256, A), jnp.float32),
            jax.ShapeDtypeStruct((128, 512), jnp.bfloat16),
        ),
        in_specs=[VMEM] * 5,
        out_specs=(VMEM, VMEM, VMEM),
        scratch_shapes=[
            pltpu.VMEM((A, A), jnp.bfloat16),
            pltpu.VMEM((256, A), jnp.bfloat16),
            pltpu.VMEM((256, A), jnp.bfloat16),
            pltpu.VMEM((A, 512), jnp.bfloat16),
            pltpu.VMEM((512, 512), jnp.bfloat16),
        ],
        compiler_params=pltpu.CompilerParams(vmem_limit_bytes=50 * 2**20),
        name="local",
    )(
        spectra,
        slot_of_antenna.reshape(16, 128),
        antenna_positions.T,
        beam_directions.T,
        jnp.asarray(steering_table()),
    )
    received = lax.all_to_all(formed, "band", split_axis=0, concat_axis=0, tiled=True)
    split_up = received.reshape(C, 2, 4, 2, 2, 32).astype(jnp.float32)
    series = jnp.einsum(
        "khsqrt,qkpn->hpstrn",
        split_up,
        jnp.asarray(inverse_table(), jnp.float32),
        precision=lax.Precision.HIGHEST,
    )
    return (real[None, None], imag[None, None], series.reshape(2, 1, 1, 2, NB * 64))


def solution(mesh):
    in_specs = (P(None, "band", "segment"), P(), P(), P())
    out_specs = (
        P("band", "segment", None, None),
        P("band", "segment", None, None),
        P(None, "segment", "band", None, None),
    )
    return jax.shard_map(
        per_device, mesh=mesh, in_specs=in_specs, out_specs=out_specs, check_vma=False
    )
```

```python
import math

import jax
import jax.numpy as jnp
import numpy as np
from jax import lax
from jax.experimental import pallas as pl
from jax.experimental.pallas import tpu as pltpu
from jax.sharding import PartitionSpec as P

A = 2048
C = 64
BEAMS = 1024
NB = 256
MESH = pl.DeviceIdType.MESH
LAG = 5


def dft_parts():
    index = np.arange(64)
    theta = (np.outer(index, index) % 64) * (2.0 * math.pi / 64.0)
    return np.cos(theta) * 0.125, np.sin(theta) * 0.125


def split(table):
    high = table.astype(np.float32).astype(jnp.bfloat16)
    low = (table - high.astype(np.float64)).astype(np.float32).astype(jnp.bfloat16)
    return high, low


def forward_tables():
    cosine, sine = dft_parts()
    parts = np.array([[cosine, -sine], [sine, cosine]])
    table = np.zeros((2, 2, 64, 2, 2, 64))
    for t1 in range(2):
        table[:, t1, :, :, t1, :] = parts.transpose(1, 3, 0, 2)
    return split(table.reshape(256, 256))


def inverse_tables():
    cosine, sine = dft_parts()
    parts = np.array([[cosine, sine], [-sine, cosine]])
    table = np.zeros((2, 2, 64, 2, 2, 64))
    for t1 in range(2):
        table[:, t1, :, :, t1, :] = parts.transpose(0, 2, 1, 3)
    return split(table.reshape(256, 256))


def steering_table():
    phase = np.arange(64) * (2.0 * math.pi / 64.0)
    row = np.concatenate([np.cos(phase), -np.sin(phase)]).astype(np.float32)
    return row.reshape(1, 128)


def place():
    segment = lax.axis_index("segment")
    band = lax.axis_index("band")
    core, half, channel = segment % 2, band % 2, band // 2
    return segment, band, core, half, channel, channel // 4, channel % 4, half * 2 + segment // 2


def offset_of(step):
    odd = step % 2
    return (8 + odd * (-(step + 1) // 2) + (1 - odd) * (step // 2)) % 16


def channelize(v_ref, high_ref, low_ref, wide, turned, spectra_f, spectra):
    for p in range(2):
        for t2 in range(32):
            wide[p, t2 * 16 : (t2 + 1) * 16, :] = v_ref[p, :, t2 * 128 : (t2 + 1) * 128].astype(
                jnp.float32
            )
    for a in range(16):
        for p in range(2):
            turned[a * 32 : (a + 1) * 32, p * 128 : (p + 1) * 128] = wide[
                p, pl.ds(a, 32, stride=16), :
            ].astype(jnp.bfloat16)
    dims = (((1,), (1,)), ((), ()))
    lane = lax.broadcasted_iota(jnp.int32, (64, 128), 1)
    first, even = lane < 64, (lane // 32) % 2 == 0
    for g in range(4):
        block = turned[g * 128 : (g + 1) * 128, :]
        out = lax.dot_general(high_ref[...], block, dims, preferred_element_type=jnp.float32)
        out += lax.dot_general(low_ref[...], block, dims, preferred_element_type=jnp.float32)
        part = [out[i * 64 : (i + 1) * 64] for i in range(4)]
        for i in range(2):
            a, b = part[i], part[i + 2]
            part[i] = jnp.where(first, a, pltpu.roll(b, 64, 1))
            part[i + 2] = jnp.where(first, pltpu.roll(a, 64, 1), b)
        for i in (0, 2):
            a, b = part[i], part[i + 1]
            part[i] = jnp.where(even, a, pltpu.roll(b, 32, 1))
            part[i + 1] = jnp.where(even, pltpu.roll(a, 96, 1), b)
        for i in range(4):
            spectra_f[pl.ds(g * 4 + i, 64, stride=16), :] = part[i]
    spectra[...] = spectra_f[...].astype(jnp.bfloat16)


def column_of(row):
    return jnp.transpose(jnp.broadcast_to(row, (128, 128)))


def build_pick(slot_ref, pick):
    lane = lax.broadcasted_iota(jnp.int32, (128, 128), 1)

    def block(r, carry):
        slot = column_of(slot_ref[pl.ds(r, 1), :])
        rows = pl.ds(pl.multiple_of(r * 128, 128), 128)
        for c in range(16):
            position = lane + c * 128
            name = ((position % 1024) // 16) * 32 + (position // 1024) * 16 + position % 16
            pick[rows, c * 128 : (c + 1) * 128] = jnp.where(slot == name, 1.0, 0.0).astype(
                jnp.bfloat16
            )
        return carry

    lax.fori_loop(0, 16, block, 0)


def build_weights(pos_ref, dir_ref, tab_ref, weight_a, half, segment, channel):
    start = pl.multiple_of(half * 512 + segment * 128, 128)
    turn0 = column_of(dir_ref[0:1, pl.ds(start, 128)]) * channel
    turn1 = column_of(dir_ref[1:2, pl.ds(start, 128)]) * channel
    table = jnp.broadcast_to(tab_ref[...], (128, 128))
    for c in range(16):
        sl = slice(c * 128, (c + 1) * 128)
        phase = (turn0 * pos_ref[0:1, sl] + turn1 * pos_ref[1:2, sl]) & 63
        weight_a[0:128, sl] = jnp.take_along_axis(table, phase, axis=1).astype(jnp.bfloat16)
        weight_a[128:256, sl] = jnp.take_along_axis(table, phase + 64, axis=1).astype(jnp.bfloat16)


def kernel(
    v_hbm, high_hbm, low_hbm, slot_hbm, pos_hbm, dir_hbm, tab_hbm,
    real_ref, imag_ref, beams_ref,
    v_ref, high_ref, low_ref, slot_ref, pos_ref, dir_ref, tab_ref,
    wide, turned, spectra_f, spectra, x_ref, pick, weight_a, weight_u, ordered, left,
    formed_f, formed,
    send_a, recv_a, send_y, recv_y, send_c, recv_c, send_b, recv_b, own_b, load,
):
    segment, band, core, half, channel, z, x, y = place()
    loads = [
        pltpu.make_async_copy(source, target, load.at[i])
        for i, (source, target) in enumerate(
            (
                (v_hbm, v_ref),
                (high_hbm, high_ref),
                (low_hbm, low_ref),
                (slot_hbm, slot_ref),
                (pos_hbm, pos_ref),
                (dir_hbm, dir_ref),
                (tab_hbm, tab_ref),
            )
        )
    ]
    for copy in loads:
        copy.start()

    def column(y_to, core_to):
        return ((y_to % 2) * 2 + core_to, channel * 2 + y_to // 2)

    up, down = (y + 1) % 4, (y + 3) % 4
    partner = column(y, 1 - core)
    barrier = pltpu.get_barrier_semaphore()

    def greet(step, carry):
        pl.semaphore_signal(
            barrier, inc=1, device_id=(segment, (band + step) % 128), device_id_type=MESH
        )
        return carry

    lax.fori_loop(1, 128, greet, 0)
    for target in (column(up, core), column(down, core), partner):
        pl.semaphore_signal(barrier, inc=1, device_id=target, device_id_type=MESH)

    for copy in loads:
        copy.wait()
    channelize(v_ref, high_ref, low_ref, wide, turned, spectra_f, spectra)
    build_pick(slot_ref, pick)
    build_weights(pos_ref, dir_ref, tab_ref, weight_a, half, segment, channel)

    pl.semaphore_wait(barrier, 130)

    def chunk(y_from, core_from, z_from, rows):
        row = pl.multiple_of((y_from // 2) * 1024 + z_from * 64, 64)
        lane = pl.multiple_of(((y_from % 2) * 2 + core_from) * 128, 128)
        return x_ref.at[pl.ds(row, rows), pl.ds(lane, 128)]

    home = x_ref.at[
        pl.ds(pl.multiple_of(half * 1024 + channel * 16, 16), 16),
        pl.ds(pl.multiple_of(segment * 128, 128), 128),
    ]

    def message(step, across):
        to = ((z + offset_of(step)) % 16) * 4 + (x + across) % 4
        return pltpu.make_async_remote_copy(
            src_ref=spectra.at[pl.ds(pl.multiple_of(to * 16, 16), 16), :],
            dst_ref=home,
            send_sem=send_a,
            recv_sem=recv_a.at[step],
            device_id=(segment, to * 2 + half),
            device_id_type=MESH,
        )

    def send(step, carry):
        for across in range(4):
            message(step, across).start()
        return carry

    lax.fori_loop(0, 15, send, 0)
    for across in range(1, 4):
        message(15, across).start()
    own = pltpu.make_async_copy(
        spectra.at[pl.ds(pl.multiple_of(channel * 16, 16), 16), :], home, recv_a.at[15]
    )
    own.start()

    def to_slots(c, carry):
        lanes = pl.ds(pl.multiple_of(c * 256, 256), 256)
        weight_u[:, lanes] = jnp.dot(
            weight_a[...], pick[:, lanes], preferred_element_type=jnp.float32
        ).astype(jnp.bfloat16)
        return carry

    lax.fori_loop(0, 8, to_slots, 0)

    def forward(y_from, step, target, send_sem, recv_sem):
        source = chunk(y_from, core, (z + 16 - offset_of(step)) % 16, 64)
        return pltpu.make_async_remote_copy(
            src_ref=source,
            dst_ref=source,
            send_sem=send_sem,
            recv_sem=recv_sem,
            device_id=target,
            device_id_type=MESH,
        )

    relay_from = (y + 3 + 2 * core) % 4
    relay_to = (y + 1 + 2 * core) % 4
    across_from = (y + 2) % 4

    def arrived(ref, sem):
        pltpu.make_async_copy(ref, ref, sem).wait()

    def to_partner(y_from, kind, step):
        forward(y_from, step, partner, send_c.at[kind], recv_c.at[kind]).start()

    def level0(step):
        arrived(chunk(y, core, (z + 16 - offset_of(step)) % 16, 64), recv_a.at[step])
        forward(y, step, column(up, core), send_y.at[0], recv_y.at[0, step]).start()
        forward(y, step, column(down, core), send_y.at[1], recv_y.at[1, step]).start()
        to_partner(y, 0, step)

    def level1(step):
        forward(down, step, partner, send_y.at[0], recv_y.at[0, step]).wait_recv()
        forward(up, step, partner, send_y.at[1], recv_y.at[1, step]).wait_recv()
        forward(relay_from, step, column(relay_to, core), send_y.at[2], recv_y.at[2, step]).start()
        to_partner(down, 1, step)
        to_partner(up, 2, step)

    def level2(step):
        forward(across_from, step, partner, send_y.at[2], recv_y.at[2, step]).wait_recv()
        to_partner(across_from, 3, step)

    def body(step, carry):
        pl.when(step < 16)(lambda: level0(step))
        pl.when((step >= LAG) & (step < 16 + LAG))(lambda: level1(step - LAG))
        pl.when(step >= 2 * LAG)(lambda: level2(step - 2 * LAG))
        return carry

    lax.fori_loop(0, 16 + 2 * LAG, body, 0)

    def plane(y_from, core_from):
        return chunk(y_from, core_from, 0, 1024)

    for kind, y_from in enumerate((y, down, up, across_from)):
        arrived(plane(y_from, 1 - core), recv_c.at[kind])

    low_lane = lax.broadcasted_iota(jnp.int32, (128, 128), 1) < 64
    beam_scale = 1.0 / math.sqrt(A)
    mixed = jnp.dot(weight_u[...], x_ref[...], preferred_element_type=jnp.float32)
    for s in range(4):
        sl = slice(s * 128, (s + 1) * 128)
        other = pltpu.roll(mixed[128:256, sl], 64, 1)
        sums = mixed[0:128, sl] + jnp.where(low_lane, -other, other)
        formed_f[pl.ds(s, 128, stride=4), :] = sums * beam_scale
    for e in range(128):
        formed[e] = formed_f[e * 4 : (e + 1) * 4, :].astype(jnp.bfloat16)

    def send_beams(step, carry):
        to = (band + 64 + step) % 128
        pltpu.make_async_remote_copy(
            src_ref=formed.at[to],
            dst_ref=beams_ref.at[band],
            send_sem=send_b,
            recv_sem=recv_b,
            device_id=(segment, to),
            device_id_type=MESH,
        ).start()
        return carry

    lax.fori_loop(0, 64, send_beams, 0)
    lax.fori_loop(65, 128, send_beams, 0)
    own_beam = pltpu.make_async_copy(formed.at[band], beams_ref.at[band], own_b)
    own_beam.start()

    def reorder(step, carry):
        rows = pl.ds(pl.multiple_of(step * 256, 256), 256)
        ordered[rows, :] = jnp.dot(
            pick[rows, :], x_ref[...], preferred_element_type=jnp.float32
        ).astype(jnp.bfloat16)
        return carry

    lax.fori_loop(0, 8, reorder, 0)

    mine = ordered[pl.ds(pl.multiple_of((half * 4 + segment) * 256, 256), 256), :]
    low_lanes = lax.broadcasted_iota(jnp.int32, (256, 128), 1) < 64
    left[0:256, :] = mine
    for s in range(4):
        sl = slice(s * 128, (s + 1) * 128)
        other = pltpu.roll(mine[:, sl].astype(jnp.float32), 64, 1)
        left[256:512, sl] = jnp.where(low_lanes, other, -other).astype(jnp.bfloat16)
    dims = (((1,), (1,)), ((), ()))

    def correlate(step, carry):
        rows = pl.ds(pl.multiple_of(step * 256, 256), 256)
        gram = lax.dot_general(left[...], ordered[rows, :], dims, preferred_element_type=jnp.float32)
        gram = gram * (1.0 / NB)
        real_ref[:, rows] = gram[0:256]
        imag_ref[:, rows] = gram[256:512]
        return carry

    lax.fori_loop(0, 8, correlate, 0)

    for kind, y_from in enumerate((y, down, up, across_from)):
        arrived(plane(y_from, core), send_c.at[kind])
    for kind in range(3):
        arrived(plane(y, core), send_y.at[kind])
    arrived(spectra.at[pl.ds(0, 63 * 16), :], send_a)
    own_beam.wait()
    arrived(formed.at[pl.ds(0, 127)], send_b)
    arrived(beams_ref.at[pl.ds(0, 127)], recv_b)


def finish_kernel(
    real_ref, imag_ref, beams_ref, high_hbm, low_hbm, real_hbm, imag_hbm, series_hbm,
    high_ref, low_ref, wide, turned, series, out_sem, load,
):
    loads = [
        pltpu.make_async_copy(high_hbm, high_ref, load.at[0]),
        pltpu.make_async_copy(low_hbm, low_ref, load.at[1]),
    ]
    for copy in loads:
        copy.start()
    copies = [
        pltpu.make_async_copy(real_ref, real_hbm.at[0, 0], out_sem.at[0]),
        pltpu.make_async_copy(imag_ref, imag_hbm.at[0, 0], out_sem.at[1]),
    ]
    for copy in copies:
        copy.start()
    for i in range(128):
        wide[i * 4 : (i + 1) * 4, :] = beams_ref[i].astype(jnp.float32)
    for h in range(2):
        for s in range(4):
            block = jnp.transpose(wide[pl.ds(h * 4 + s, 64, stride=8), :])
            for part in range(4):
                turned[h * 128 + s * 32 : h * 128 + (s + 1) * 32, part * 64 : (part + 1) * 64] = block[
                    part * 32 : (part + 1) * 32
                ].astype(jnp.bfloat16)
    for copy in loads:
        copy.wait()
    out = jnp.dot(turned[...], high_ref[...], preferred_element_type=jnp.float32)
    out += jnp.dot(turned[...], low_ref[...], preferred_element_type=jnp.float32)
    for h in range(2):
        for q in range(2):
            series[pl.ds(h * 256 + q, 128, stride=2), :] = out[
                h * 128 : (h + 1) * 128, q * 128 : (q + 1) * 128
            ]
    copies.append(pltpu.make_async_copy(series, series_hbm, out_sem.at[2]))
    copies[2].start()
    for copy in copies:
        copy.wait()


VMEM = pl.BlockSpec(memory_space=pltpu.VMEM)
HBM = pl.BlockSpec(memory_space=pltpu.HBM)


def in_hbm(array):
    return pltpu.with_memory_space_constraint(array, pltpu.HBM)


def per_device(voltages, slot_of_antenna, antenna_positions, beam_directions):
    high, low = forward_tables()
    real, imag, received = pl.pallas_call(
        kernel,
        out_shape=(
            jax.ShapeDtypeStruct((256, A), jnp.float32),
            jax.ShapeDtypeStruct((256, A), jnp.float32),
            jax.ShapeDtypeStruct((128, 4, 128), jnp.bfloat16),
        ),
        in_specs=[HBM] * 7,
        out_specs=(VMEM, VMEM, VMEM),
        scratch_shapes=[
            pltpu.VMEM((2, 16, 4096), jnp.bfloat16),
            pltpu.VMEM((256, 256), jnp.bfloat16),
            pltpu.VMEM((256, 256), jnp.bfloat16),
            pltpu.VMEM((16, 128), jnp.int32),
            pltpu.VMEM((2, A), jnp.int32),
            pltpu.VMEM((2, BEAMS), jnp.int32),
            pltpu.VMEM((1, 128), jnp.float32),
            pltpu.VMEM((2, 512, 128), jnp.float32),
            pltpu.VMEM((512, 256), jnp.bfloat16),
            pltpu.VMEM((1024, 128), jnp.float32),
            pltpu.VMEM((1024, 128), jnp.bfloat16),
            pltpu.VMEM((A, 512), jnp.bfloat16),
            pltpu.VMEM((A, A), jnp.bfloat16),
            pltpu.VMEM((256, A), jnp.bfloat16),
            pltpu.VMEM((256, A), jnp.bfloat16),
            pltpu.VMEM((A, 512), jnp.bfloat16),
            pltpu.VMEM((512, 512), jnp.bfloat16),
            pltpu.VMEM((512, 128), jnp.float32),
            pltpu.VMEM((128, 4, 128), jnp.bfloat16),
            pltpu.SemaphoreType.DMA,
            pltpu.SemaphoreType.DMA((16,)),
            pltpu.SemaphoreType.DMA((3,)),
            pltpu.SemaphoreType.DMA((3, 16)),
            pltpu.SemaphoreType.DMA((4,)),
            pltpu.SemaphoreType.DMA((4,)),
            pltpu.SemaphoreType.DMA,
            pltpu.SemaphoreType.DMA,
            pltpu.SemaphoreType.DMA,
            pltpu.SemaphoreType.DMA((7,)),
        ],
        compiler_params=pltpu.CompilerParams(
            collective_id=0, has_side_effects=True, vmem_limit_bytes=32 * 2**20
        ),
        name="correlator",
    )(
        *(
            in_hbm(array)
            for array in (
                voltages,
                jnp.asarray(high),
                jnp.asarray(low),
                slot_of_antenna.reshape(16, 128),
                antenna_positions.T,
                beam_directions.T,
                jnp.asarray(steering_table()),
            )
        )
    )
    inverse_high, inverse_low = inverse_tables()
    real, imag, series = pl.pallas_call(
        finish_kernel,
        out_shape=(
            jax.ShapeDtypeStruct((1, 1, 256, A), jnp.float32),
            jax.ShapeDtypeStruct((1, 1, 256, A), jnp.float32),
            jax.ShapeDtypeStruct((512, 128), jnp.float32),
        ),
        in_specs=[VMEM] * 3 + [HBM] * 2,
        out_specs=[HBM] * 3,
        scratch_shapes=[
            pltpu.VMEM((256, 256), jnp.bfloat16),
            pltpu.VMEM((256, 256), jnp.bfloat16),
            pltpu.VMEM((512, 128), jnp.float32),
            pltpu.VMEM((256, 256), jnp.bfloat16),
            pltpu.VMEM((512, 128), jnp.float32),
            pltpu.SemaphoreType.DMA((3,)),
            pltpu.SemaphoreType.DMA((2,)),
        ],
        compiler_params=pltpu.CompilerParams(vmem_limit_bytes=16 * 2**20),
        name="finish",
    )(
        real,
        imag,
        received,
        in_hbm(jnp.asarray(inverse_high)),
        in_hbm(jnp.asarray(inverse_low)),
    )
    series = series.reshape(2, 128, 2, 128).transpose(0, 2, 1, 3).reshape(2, 1, 1, 2, NB * 64)
    return (real, imag, series)


def solution(mesh):
    in_specs = (P(None, "band", "segment"), P(), P(), P())
    out_specs = (
        P("band", "segment", None, None),
        P("band", "segment", None, None),
        P(None, "segment", "band", None, None),
    )
    return jax.shard_map(
        per_device, mesh=mesh, in_specs=in_specs, out_specs=out_specs, check_vma=False
    )
```

```python
import math

import jax
import jax.numpy as jnp
import numpy as np
from jax import lax
from jax.experimental import pallas as pl
from jax.experimental.pallas import tpu as pltpu
from jax.sharding import PartitionSpec as P

A = 2048
C = 64
BEAMS = 1024
NB = 256
MESH = pl.DeviceIdType.MESH
LAG1 = 5
LAG2 = 10


def dft_parts():
    index = np.arange(64)
    theta = (np.outer(index, index) % 64) * (2.0 * math.pi / 64.0)
    return np.cos(theta) * 0.125, np.sin(theta) * 0.125


def split(table):
    high = table.astype(np.float32).astype(jnp.bfloat16)
    low = (table - high.astype(np.float64)).astype(np.float32).astype(jnp.bfloat16)
    return high, low


def forward_tables():
    cosine, sine = dft_parts()
    parts = np.array([[cosine, -sine], [sine, cosine]])
    table = np.zeros((2, 2, 64, 2, 2, 64))
    for t1 in range(2):
        table[:, t1, :, :, t1, :] = parts.transpose(1, 3, 0, 2)
    return split(table.reshape(256, 256))


def inverse_tables():
    cosine, sine = dft_parts()
    parts = np.array([[cosine, sine], [-sine, cosine]])
    table = np.zeros((2, 2, 64, 2, 2, 64))
    for t1 in range(2):
        table[:, t1, :, :, t1, :] = parts.transpose(0, 2, 1, 3)
    return split(table.reshape(256, 256))


def steering_table():
    phase = np.arange(64) * (2.0 * math.pi / 64.0)
    row = np.concatenate([np.cos(phase), -np.sin(phase)]).astype(np.float32)
    return row.reshape(1, 128)


def place():
    segment = lax.axis_index("segment")
    band = lax.axis_index("band")
    core, half, channel = segment % 2, band % 2, band // 2
    return segment, band, core, half, channel, channel // 4, channel % 4, half * 2 + segment // 2


def offset_of(step):
    odd = step % 2
    return (odd * ((step + 1) // 2) + (1 - odd) * (16 - step // 2)) % 16


def far_offset(step):
    odd = step % 2
    return (8 - odd * ((step + 1) // 2) + (1 - odd) * (step // 2)) % 16


def channelize(v_ref, high_ref, low_ref, wide, turned, spectra_f, spectra):
    for p in range(2):
        for t2 in range(32):
            wide[p, t2 * 16 : (t2 + 1) * 16, :] = v_ref[p, :, t2 * 128 : (t2 + 1) * 128].astype(
                jnp.float32
            )
    for a in range(16):
        for p in range(2):
            turned[a * 32 : (a + 1) * 32, p * 128 : (p + 1) * 128] = wide[
                p, pl.ds(a, 32, stride=16), :
            ].astype(jnp.bfloat16)
    dims = (((1,), (1,)), ((), ()))
    lane = lax.broadcasted_iota(jnp.int32, (64, 128), 1)
    first, even = lane < 64, (lane // 32) % 2 == 0
    for g in range(4):
        block = turned[g * 128 : (g + 1) * 128, :]
        out = lax.dot_general(high_ref[...], block, dims, preferred_element_type=jnp.float32)
        out += lax.dot_general(low_ref[...], block, dims, preferred_element_type=jnp.float32)
        part = [out[i * 64 : (i + 1) * 64] for i in range(4)]
        for i in range(2):
            a, b = part[i], part[i + 2]
            part[i] = jnp.where(first, a, pltpu.roll(b, 64, 1))
            part[i + 2] = jnp.where(first, pltpu.roll(a, 64, 1), b)
        for i in (0, 2):
            a, b = part[i], part[i + 1]
            part[i] = jnp.where(even, a, pltpu.roll(b, 32, 1))
            part[i + 1] = jnp.where(even, pltpu.roll(a, 96, 1), b)
        for i in range(4):
            spectra_f[pl.ds(g * 4 + i, 64, stride=16), :] = part[i]
    spectra[...] = spectra_f[...].astype(jnp.bfloat16)


def column_of(row):
    return jnp.transpose(jnp.broadcast_to(row, (128, 128)))


def build_pick(slot_ref, pick, r):
    lane = lax.broadcasted_iota(jnp.int32, (128, 128), 1)
    slot = column_of(slot_ref[pl.ds(r, 1), :])
    rows = pl.ds(pl.multiple_of(r * 128, 128), 128)
    for c in range(16):
        position = lane + c * 128
        name = ((position % 1024) // 16) * 32 + (position // 1024) * 16 + position % 16
        pick[rows, c * 128 : (c + 1) * 128] = jnp.where(slot == name, 1.0, 0.0).astype(jnp.bfloat16)


def build_weights(pos_ref, turn, tab_ref, weight_a, c):
    table = jnp.broadcast_to(tab_ref[...], (128, 128))
    lanes = pl.ds(pl.multiple_of(c * 128, 128), 128)
    phase = (turn[0] * pos_ref[0:1, lanes] + turn[1] * pos_ref[1:2, lanes]) & 63
    weight_a[0:128, lanes] = jnp.take_along_axis(table, phase, axis=1).astype(jnp.bfloat16)
    weight_a[128:256, lanes] = jnp.take_along_axis(table, phase + 64, axis=1).astype(jnp.bfloat16)


def kernel(
    v_hbm, high_hbm, low_hbm, slot_hbm, pos_hbm, dir_hbm, tab_hbm,
    real_ref, imag_ref, beams_ref,
    v_ref, high_ref, low_ref, slot_ref, pos_ref, dir_ref, tab_ref,
    wide, turned, spectra_f, spectra, x_ref, pick, weight_a, weight_u, ordered, left,
    formed_f, formed,
    send_a, recv_a, send_y, recv_y, send_c, recv_c, send_b, recv_b, own_b, load, from_above, from_below,
):
    segment, band, core, half, channel, z, x, y = place()
    loads = [
        pltpu.make_async_copy(source, target, load.at[i])
        for i, (source, target) in enumerate(
            (
                (v_hbm, v_ref),
                (high_hbm, high_ref),
                (low_hbm, low_ref),
                (slot_hbm, slot_ref),
                (pos_hbm, pos_ref),
                (dir_hbm, dir_ref),
                (tab_hbm, tab_ref),
            )
        )
    ]
    for copy in loads:
        copy.start()

    def column(y_to, core_to):
        return ((y_to % 2) * 2 + core_to, channel * 2 + y_to // 2)

    up, down = (y + 1) % 4, (y + 3) % 4
    partner = column(y, 1 - core)
    barrier = pltpu.get_barrier_semaphore()

    above, below = ((z + 1) % 16) * 4 + x, ((z + 15) % 16) * 4 + x

    def beside(other):
        return (segment, other * 2 + half)

    greeted = [beside(z * 4 + (x + across) % 4) for across in range(1, 4)]
    greeted += [beside(above), beside(below), column(up, core), column(down, core), partner]
    for target in greeted:
        pl.semaphore_signal(barrier, inc=1, device_id=target, device_id_type=MESH)

    for copy in loads:
        copy.wait()
    channelize(v_ref, high_ref, low_ref, wide, turned, spectra_f, spectra)
    pl.semaphore_wait(barrier, 8)

    def tell(sem, target):
        pl.semaphore_signal(sem, inc=1, device_id=beside(target), device_id_type=MESH)

    tell(from_above, below)
    tell(from_below, above)

    def chunk(y_from, core_from, z_from, rows):
        row = pl.multiple_of((y_from // 2) * 1024 + z_from * 64, 64)
        lane = pl.multiple_of(((y_from % 2) * 2 + core_from) * 128, 128)
        return x_ref.at[pl.ds(row, rows), pl.ds(lane, 128)]

    home = x_ref.at[
        pl.ds(pl.multiple_of(half * 1024 + channel * 16, 16), 16),
        pl.ds(pl.multiple_of(segment * 128, 128), 128),
    ]

    def message(step, across):
        to = ((z + offset_of(step)) % 16) * 4 + (x + across) % 4
        return pltpu.make_async_remote_copy(
            src_ref=spectra.at[pl.ds(pl.multiple_of(to * 16, 16), 16), :],
            dst_ref=home,
            send_sem=send_a,
            recv_sem=recv_a.at[step],
            device_id=(segment, to * 2 + half),
            device_id_type=MESH,
        )

    own = pltpu.make_async_copy(
        spectra.at[pl.ds(pl.multiple_of(channel * 16, 16), 16), :], home, recv_a.at[0]
    )
    own.start()
    for across in range(1, 4):
        message(0, across).start()
    start = pl.multiple_of(half * 512 + segment * 128, 128)
    turn = [column_of(dir_ref[i : i + 1, pl.ds(start, 128)]) * channel for i in range(2)]

    def reach(d, carry):
        pl.semaphore_wait(from_above, 1)
        tell(from_above, below)
        for across in range(4):
            message(2 * d - 1, across).start()
        pl.semaphore_wait(from_below, 1)
        pl.when(d < 7)(lambda: tell(from_below, above))
        for across in range(4):
            message(2 * d, across).start()
        for i in range(2):
            build_pick(slot_ref, pick, 2 * d - 2 + i)
            build_weights(pos_ref, turn, tab_ref, weight_a, 2 * d - 2 + i)
        return carry

    lax.fori_loop(1, 8, reach, 0)
    pl.semaphore_wait(from_above, 1)
    for across in range(4):
        message(15, across).start()
    for i in range(14, 16):
        build_pick(slot_ref, pick, i)
        build_weights(pos_ref, turn, tab_ref, weight_a, i)

    def to_slots(c):
        lanes = pl.ds(pl.multiple_of(c * 256, 256), 256)
        weight_u[:, lanes] = jnp.dot(
            weight_a[...], pick[:, lanes], preferred_element_type=jnp.float32
        ).astype(jnp.bfloat16)

    def forward(y_from, step, target, send_sem, recv_sem):
        source = chunk(y_from, core, (z + 16 - offset_of(step)) % 16, 64)
        return pltpu.make_async_remote_copy(
            src_ref=source,
            dst_ref=source,
            send_sem=send_sem,
            recv_sem=recv_sem,
            device_id=target,
            device_id_type=MESH,
        )

    relay_from = (y + 3 + 2 * core) % 4
    relay_to = (y + 1 + 2 * core) % 4
    across_from = (y + 2) % 4

    def arrived(ref, sem):
        pltpu.make_async_copy(ref, ref, sem).wait()

    def to_partner(y_from, kind, step):
        forward(y_from, step, partner, send_c.at[kind], recv_c.at[kind]).start()

    def level0(step):
        arrived(chunk(y, core, (z + 16 - offset_of(step)) % 16, 64), recv_a.at[step])
        forward(y, step, column(up, core), send_y.at[0], recv_y.at[0, step]).start()
        forward(y, step, column(down, core), send_y.at[1], recv_y.at[1, step]).start()
        to_partner(y, 0, step)

    def level1(step):
        forward(down, step, partner, send_y.at[0], recv_y.at[0, step]).wait_recv()
        forward(up, step, partner, send_y.at[1], recv_y.at[1, step]).wait_recv()
        forward(relay_from, step, column(relay_to, core), send_y.at[2], recv_y.at[2, step]).start()
        to_partner(down, 1, step)
        to_partner(up, 2, step)

    def level2(step):
        forward(across_from, step, partner, send_y.at[2], recv_y.at[2, step]).wait_recv()
        to_partner(across_from, 3, step)

    def body(step, carry):
        pl.when(step < 16)(lambda: level0(step))
        pl.when((step >= LAG1) & (step < 16 + LAG1))(lambda: level1(step - LAG1))
        pl.when(step >= LAG2)(lambda: level2(step - LAG2))
        pl.when((step >= 4) & (step < 12))(lambda: to_slots(step - 4))
        return carry

    lax.fori_loop(0, 16 + LAG2, body, 0)

    def plane(y_from, core_from):
        return chunk(y_from, core_from, 0, 1024)

    for kind, y_from in enumerate((y, down, up, across_from)):
        arrived(plane(y_from, 1 - core), recv_c.at[kind])

    low_lane = lax.broadcasted_iota(jnp.int32, (128, 128), 1) < 64
    beam_scale = 1.0 / math.sqrt(A)
    mixed = jnp.dot(weight_u[...], x_ref[...], preferred_element_type=jnp.float32)
    for s in range(4):
        sl = slice(s * 128, (s + 1) * 128)
        other = pltpu.roll(mixed[128:256, sl], 64, 1)
        sums = mixed[0:128, sl] + jnp.where(low_lane, -other, other)
        formed_f[pl.ds(s, 128, stride=4), :] = sums * beam_scale
    for e in range(128):
        formed[e] = formed_f[e * 4 : (e + 1) * 4, :].astype(jnp.bfloat16)

    def send_beam(step, turn_by):
        to = ((z + far_offset(step)) % 16) * 8 + (band % 8 + turn_by) % 8
        pltpu.make_async_remote_copy(
            src_ref=formed.at[to],
            dst_ref=beams_ref.at[band],
            send_sem=send_b,
            recv_sem=recv_b,
            device_id=(segment, to),
            device_id_type=MESH,
        ).start()

    def send_beams(step, carry):
        for turn_by in range(8):
            send_beam(step, turn_by)
        return carry

    lax.fori_loop(0, 15, send_beams, 0)
    for turn_by in range(1, 8):
        send_beam(15, turn_by)
    own_beam = pltpu.make_async_copy(formed.at[band], beams_ref.at[band], own_b)
    own_beam.start()

    def reorder(step, carry):
        rows = pl.ds(pl.multiple_of(step * 256, 256), 256)
        ordered[rows, :] = jnp.dot(
            pick[rows, :], x_ref[...], preferred_element_type=jnp.float32
        ).astype(jnp.bfloat16)
        return carry

    lax.fori_loop(0, 8, reorder, 0)

    mine = ordered[pl.ds(pl.multiple_of((half * 4 + segment) * 256, 256), 256), :]
    low_lanes = lax.broadcasted_iota(jnp.int32, (256, 128), 1) < 64
    left[0:256, :] = mine
    for s in range(4):
        sl = slice(s * 128, (s + 1) * 128)
        other = pltpu.roll(mine[:, sl].astype(jnp.float32), 64, 1)
        left[256:512, sl] = jnp.where(low_lanes, other, -other).astype(jnp.bfloat16)
    dims = (((1,), (1,)), ((), ()))

    def correlate(step, carry):
        rows = pl.ds(pl.multiple_of(step * 256, 256), 256)
        gram = lax.dot_general(left[...], ordered[rows, :], dims, preferred_element_type=jnp.float32)
        gram = gram * (1.0 / NB)
        real_ref[:, rows] = gram[0:256]
        imag_ref[:, rows] = gram[256:512]
        return carry

    lax.fori_loop(0, 8, correlate, 0)

    for kind, y_from in enumerate((y, down, up, across_from)):
        arrived(plane(y_from, core), send_c.at[kind])
    for kind in range(3):
        arrived(plane(y, core), send_y.at[kind])
    arrived(spectra.at[pl.ds(0, 63 * 16), :], send_a)
    own_beam.wait()
    arrived(formed.at[pl.ds(0, 127)], send_b)
    arrived(beams_ref.at[pl.ds(0, 127)], recv_b)


def finish_kernel(
    real_ref, imag_ref, beams_ref, high_hbm, low_hbm, real_hbm, imag_hbm, series_hbm,
    high_ref, low_ref, wide, turned, series, out_sem, load,
):
    loads = [
        pltpu.make_async_copy(high_hbm, high_ref, load.at[0]),
        pltpu.make_async_copy(low_hbm, low_ref, load.at[1]),
    ]
    for copy in loads:
        copy.start()
    copies = [
        pltpu.make_async_copy(real_ref, real_hbm.at[0, 0], out_sem.at[0]),
        pltpu.make_async_copy(imag_ref, imag_hbm.at[0, 0], out_sem.at[1]),
    ]
    for copy in copies:
        copy.start()
    for i in range(128):
        wide[i * 4 : (i + 1) * 4, :] = beams_ref[i].astype(jnp.float32)
    for h in range(2):
        for s in range(4):
            block = jnp.transpose(wide[pl.ds(h * 4 + s, 64, stride=8), :])
            for part in range(4):
                turned[h * 128 + s * 32 : h * 128 + (s + 1) * 32, part * 64 : (part + 1) * 64] = block[
                    part * 32 : (part + 1) * 32
                ].astype(jnp.bfloat16)
    for copy in loads:
        copy.wait()
    out = jnp.dot(turned[...], high_ref[...], preferred_element_type=jnp.float32)
    out += jnp.dot(turned[...], low_ref[...], preferred_element_type=jnp.float32)
    for h in range(2):
        for q in range(2):
            series[pl.ds(h * 256 + q, 128, stride=2), :] = out[
                h * 128 : (h + 1) * 128, q * 128 : (q + 1) * 128
            ]
    copies.append(pltpu.make_async_copy(series, series_hbm, out_sem.at[2]))
    copies[2].start()
    for copy in copies:
        copy.wait()


VMEM = pl.BlockSpec(memory_space=pltpu.VMEM)
HBM = pl.BlockSpec(memory_space=pltpu.HBM)


def in_hbm(array):
    return pltpu.with_memory_space_constraint(array, pltpu.HBM)


def per_device(voltages, slot_of_antenna, antenna_positions, beam_directions):
    high, low = forward_tables()
    real, imag, received = pl.pallas_call(
        kernel,
        out_shape=(
            jax.ShapeDtypeStruct((256, A), jnp.float32),
            jax.ShapeDtypeStruct((256, A), jnp.float32),
            jax.ShapeDtypeStruct((128, 4, 128), jnp.bfloat16),
        ),
        in_specs=[HBM] * 7,
        out_specs=(VMEM, VMEM, VMEM),
        scratch_shapes=[
            pltpu.VMEM((2, 16, 4096), jnp.bfloat16),
            pltpu.VMEM((256, 256), jnp.bfloat16),
            pltpu.VMEM((256, 256), jnp.bfloat16),
            pltpu.VMEM((16, 128), jnp.int32),
            pltpu.VMEM((2, A), jnp.int32),
            pltpu.VMEM((2, BEAMS), jnp.int32),
            pltpu.VMEM((1, 128), jnp.float32),
            pltpu.VMEM((2, 512, 128), jnp.float32),
            pltpu.VMEM((512, 256), jnp.bfloat16),
            pltpu.VMEM((1024, 128), jnp.float32),
            pltpu.VMEM((1024, 128), jnp.bfloat16),
            pltpu.VMEM((A, 512), jnp.bfloat16),
            pltpu.VMEM((A, A), jnp.bfloat16),
            pltpu.VMEM((256, A), jnp.bfloat16),
            pltpu.VMEM((256, A), jnp.bfloat16),
            pltpu.VMEM((A, 512), jnp.bfloat16),
            pltpu.VMEM((512, 512), jnp.bfloat16),
            pltpu.VMEM((512, 128), jnp.float32),
            pltpu.VMEM((128, 4, 128), jnp.bfloat16),
            pltpu.SemaphoreType.DMA,
            pltpu.SemaphoreType.DMA((16,)),
            pltpu.SemaphoreType.DMA((3,)),
            pltpu.SemaphoreType.DMA((3, 16)),
            pltpu.SemaphoreType.DMA((4,)),
            pltpu.SemaphoreType.DMA((4,)),
            pltpu.SemaphoreType.DMA,
            pltpu.SemaphoreType.DMA,
            pltpu.SemaphoreType.DMA,
            pltpu.SemaphoreType.DMA((7,)),
            pltpu.SemaphoreType.REGULAR,
            pltpu.SemaphoreType.REGULAR,
        ],
        compiler_params=pltpu.CompilerParams(
            collective_id=0, has_side_effects=True, vmem_limit_bytes=32 * 2**20
        ),
        name="correlator",
    )(
        *(
            in_hbm(array)
            for array in (
                voltages,
                jnp.asarray(high),
                jnp.asarray(low),
                slot_of_antenna.reshape(16, 128),
                antenna_positions.T,
                beam_directions.T,
                jnp.asarray(steering_table()),
            )
        )
    )
    inverse_high, inverse_low = inverse_tables()
    real, imag, series = pl.pallas_call(
        finish_kernel,
        out_shape=(
            jax.ShapeDtypeStruct((1, 1, 256, A), jnp.float32),
            jax.ShapeDtypeStruct((1, 1, 256, A), jnp.float32),
            jax.ShapeDtypeStruct((512, 128), jnp.float32),
        ),
        in_specs=[VMEM] * 3 + [HBM] * 2,
        out_specs=[HBM] * 3,
        scratch_shapes=[
            pltpu.VMEM((256, 256), jnp.bfloat16),
            pltpu.VMEM((256, 256), jnp.bfloat16),
            pltpu.VMEM((512, 128), jnp.float32),
            pltpu.VMEM((256, 256), jnp.bfloat16),
            pltpu.VMEM((512, 128), jnp.float32),
            pltpu.SemaphoreType.DMA((3,)),
            pltpu.SemaphoreType.DMA((2,)),
        ],
        compiler_params=pltpu.CompilerParams(vmem_limit_bytes=16 * 2**20),
        name="finish",
    )(
        real,
        imag,
        received,
        in_hbm(jnp.asarray(inverse_high)),
        in_hbm(jnp.asarray(inverse_low)),
    )
    series = series.reshape(2, 128, 2, 128).transpose(0, 2, 1, 3).reshape(2, 1, 1, 2, NB * 64)
    return (real, imag, series)


def solution(mesh):
    in_specs = (P(None, "band", "segment"), P(), P(), P())
    out_specs = (
        P("band", "segment", None, None),
        P("band", "segment", None, None),
        P(None, "segment", "band", None, None),
    )
    return jax.shard_map(
        per_device, mesh=mesh, in_specs=in_specs, out_specs=out_specs, check_vma=False
    )
```

```python
import math

import jax
import jax.numpy as jnp
import numpy as np
from jax import lax
from jax.experimental import pallas as pl
from jax.experimental.pallas import tpu as pltpu
from jax.sharding import PartitionSpec as P

A = 2048
C = 64
BEAMS = 1024
NB = 256
MESH = pl.DeviceIdType.MESH
LAG1 = 8
LAG2 = 8
NEAR = 7
FAR = 2 * NEAR + 1
DIRECT = 0
BOTH = 13


def dft_parts():
    index = np.arange(64)
    theta = (np.outer(index, index) % 64) * (2.0 * math.pi / 64.0)
    return np.cos(theta) * 0.125, np.sin(theta) * 0.125


def split(table):
    high = table.astype(np.float32).astype(jnp.bfloat16)
    low = (table - high.astype(np.float64)).astype(np.float32).astype(jnp.bfloat16)
    return high, low


def forward_tables():
    cosine, sine = dft_parts()
    parts = np.array([[cosine, -sine], [sine, cosine]])
    table = np.zeros((2, 2, 64, 2, 2, 64))
    for t1 in range(2):
        table[:, t1, :, :, t1, :] = parts.transpose(1, 3, 0, 2)
    return split(table.reshape(256, 256))


def inverse_tables():
    cosine, sine = dft_parts()
    parts = np.array([[cosine, sine], [-sine, cosine]])
    table = np.zeros((2, 2, 64, 2, 2, 64))
    for t1 in range(2):
        table[:, t1, :, :, t1, :] = parts.transpose(0, 2, 1, 3)
    return split(table.reshape(256, 256))


def steering_table():
    phase = np.arange(64) * (2.0 * math.pi / 64.0)
    row = np.concatenate([np.cos(phase), -np.sin(phase)]).astype(np.float32)
    return row.reshape(1, 128)


def place():
    segment = lax.axis_index("segment")
    band = lax.axis_index("band")
    core, half, channel = segment % 2, band % 2, band // 2
    return segment, band, core, half, channel, channel // 4, channel % 4, half * 2 + segment // 2


def near_offset(step):
    odd = step % 2
    return (odd * ((step + 1) // 2) + (1 - odd) * (16 - step // 2)) % 16


def far_offset(step):
    odd = step % 2
    return (8 - odd * ((step + 1) // 2) + (1 - odd) * (step // 2)) % 16


def offset_of(step):
    return jnp.where(step < FAR, near_offset(step), far_offset(jnp.maximum(step - FAR, 0)))


def channelize(v_ref, high_ref, low_ref, wide, turned, spectra_f, spectra):
    for p in range(2):
        for t2 in range(32):
            wide[p, t2 * 16 : (t2 + 1) * 16, :] = v_ref[p, :, t2 * 128 : (t2 + 1) * 128].astype(
                jnp.float32
            )
    for a in range(16):
        for p in range(2):
            turned[a * 32 : (a + 1) * 32, p * 128 : (p + 1) * 128] = wide[
                p, pl.ds(a, 32, stride=16), :
            ].astype(jnp.bfloat16)
    dims = (((1,), (1,)), ((), ()))
    lane = lax.broadcasted_iota(jnp.int32, (64, 128), 1)
    first, even = lane < 64, (lane // 32) % 2 == 0
    for g in range(4):
        block = turned[g * 128 : (g + 1) * 128, :]
        out = lax.dot_general(high_ref[...], block, dims, preferred_element_type=jnp.float32)
        out += lax.dot_general(low_ref[...], block, dims, preferred_element_type=jnp.float32)
        part = [out[i * 64 : (i + 1) * 64] for i in range(4)]
        for i in range(2):
            a, b = part[i], part[i + 2]
            part[i] = jnp.where(first, a, pltpu.roll(b, 64, 1))
            part[i + 2] = jnp.where(first, pltpu.roll(a, 64, 1), b)
        for i in (0, 2):
            a, b = part[i], part[i + 1]
            part[i] = jnp.where(even, a, pltpu.roll(b, 32, 1))
            part[i + 1] = jnp.where(even, pltpu.roll(a, 96, 1), b)
        for i in range(4):
            spectra_f[pl.ds(g * 4 + i, 64, stride=16), :] = part[i]
    spectra[...] = spectra_f[...].astype(jnp.bfloat16)


def column_of(row):
    return jnp.transpose(jnp.broadcast_to(row, (128, 128)))


def build_pick(slot_ref, pick, r):
    lane = lax.broadcasted_iota(jnp.int32, (128, 128), 1)
    slot = column_of(slot_ref[pl.ds(r, 1), :])
    rows = pl.ds(pl.multiple_of(r * 128, 128), 128)
    for c in range(16):
        position = lane + c * 128
        name = ((position % 1024) // 16) * 32 + (position // 1024) * 16 + position % 16
        pick[rows, c * 128 : (c + 1) * 128] = jnp.where(slot == name, 1.0, 0.0).astype(jnp.bfloat16)


def build_weights(pos_ref, turn, tab_ref, weight_a, c):
    table = jnp.broadcast_to(tab_ref[...], (128, 128))
    lanes = pl.ds(pl.multiple_of(c * 128, 128), 128)
    phase = (turn[0] * pos_ref[0:1, lanes] + turn[1] * pos_ref[1:2, lanes]) & 63
    weight_a[0:128, lanes] = jnp.take_along_axis(table, phase, axis=1).astype(jnp.bfloat16)
    weight_a[128:256, lanes] = jnp.take_along_axis(table, phase + 64, axis=1).astype(jnp.bfloat16)


def kernel(
    v_hbm, high_hbm, low_hbm, slot_hbm, pos_hbm, dir_hbm, tab_hbm,
    real_ref, imag_ref, beams_ref,
    v_ref, high_ref, low_ref, slot_ref, pos_ref, dir_ref, tab_ref,
    wide, turned, spectra_f, spectra, x_ref, pick, weight_a, weight_u, ordered, left,
    formed_f, formed,
    send_a, recv_a, send_y, recv_y, send_c, recv_c, send_b, recv_b, own_b, load, from_above, from_below,
):
    segment, band, core, half, channel, z, x, y = place()
    loads = [
        pltpu.make_async_copy(source, target, load.at[i])
        for i, (source, target) in enumerate(
            (
                (v_hbm, v_ref),
                (high_hbm, high_ref),
                (low_hbm, low_ref),
                (slot_hbm, slot_ref),
                (pos_hbm, pos_ref),
                (dir_hbm, dir_ref),
                (tab_hbm, tab_ref),
            )
        )
    ]
    for copy in loads:
        copy.start()

    def column(y_to, core_to):
        return ((y_to % 2) * 2 + core_to, channel * 2 + y_to // 2)

    up, down = (y + 1) % 4, (y + 3) % 4
    partner = column(y, 1 - core)
    barrier = pltpu.get_barrier_semaphore()

    above, below = ((z + 1) % 16) * 4 + x, ((z + 15) % 16) * 4 + x

    def beside(other):
        return (segment, other * 2 + half)

    greeted = [beside(z * 4 + (x + across) % 4) for across in range(1, 4)]
    greeted += [beside(above), beside(below), column(up, core), column(down, core), partner]
    greeted += [column((y + 2) % 4, core), column((y + 2) % 4, 1 - core)]
    greeted += [column(up, 1 - core), column(down, 1 - core)]
    for target in greeted:
        pl.semaphore_signal(barrier, inc=1, device_id=target, device_id_type=MESH)

    for copy in loads:
        copy.wait()
    channelize(v_ref, high_ref, low_ref, wide, turned, spectra_f, spectra)
    pl.semaphore_wait(barrier, 12)

    def tell(sem, target):
        pl.semaphore_signal(sem, inc=1, device_id=beside(target), device_id_type=MESH)

    tell(from_above, below)
    tell(from_below, above)

    def chunk(y_from, core_from, z_from, rows):
        row = pl.multiple_of((y_from // 2) * 1024 + z_from * 64, 64)
        lane = pl.multiple_of(((y_from % 2) * 2 + core_from) * 128, 128)
        return x_ref.at[pl.ds(row, rows), pl.ds(lane, 128)]

    home = x_ref.at[
        pl.ds(pl.multiple_of(half * 1024 + channel * 16, 16), 16),
        pl.ds(pl.multiple_of(segment * 128, 128), 128),
    ]

    def message(step, across):
        to = ((z + offset_of(step)) % 16) * 4 + (x + across) % 4
        return pltpu.make_async_remote_copy(
            src_ref=spectra.at[pl.ds(pl.multiple_of(to * 16, 16), 16), :],
            dst_ref=home,
            send_sem=send_a,
            recv_sem=recv_a.at[step],
            device_id=(segment, to * 2 + half),
            device_id_type=MESH,
        )

    own = pltpu.make_async_copy(
        spectra.at[pl.ds(pl.multiple_of(channel * 16, 16), 16), :], home, recv_a.at[0]
    )
    own.start()
    for across in range(1, 4):
        message(0, across).start()
    start = pl.multiple_of(half * 512 + segment * 128, 128)
    turn = [column_of(dir_ref[i : i + 1, pl.ds(start, 128)]) * channel for i in range(2)]

    def reach(d, carry):
        pl.semaphore_wait(from_above, 1)
        tell(from_above, below)
        pl.semaphore_wait(from_below, 1)
        pl.when(d < 7)(lambda: tell(from_below, above))

        @pl.when(d <= NEAR)
        def _():
            for across in range(4):
                message(2 * d - 1, across).start()
            for across in range(4):
                message(2 * d, across).start()

        return carry

    lax.fori_loop(1, 8, reach, 0)
    pl.semaphore_wait(from_above, 1)

    def send_far(step, carry):
        for across in range(4):
            message(step, across).start()
        return carry

    lax.fori_loop(FAR, 16, send_far, 0)

    def prepare(step):
        for i in range(2):
            build_pick(slot_ref, pick, 2 * step + i)
            build_weights(pos_ref, turn, tab_ref, weight_a, 2 * step + i)

    def to_slots(c):
        lanes = pl.ds(pl.multiple_of(c * 256, 256), 256)
        weight_u[:, lanes] = jnp.dot(
            weight_a[...], pick[:, lanes], preferred_element_type=jnp.float32
        ).astype(jnp.bfloat16)

    def forward(y_from, step, target, send_sem, recv_sem):
        source = chunk(y_from, core, (z + 16 - offset_of(step)) % 16, 64)
        return pltpu.make_async_remote_copy(
            src_ref=source,
            dst_ref=source,
            send_sem=send_sem,
            recv_sem=recv_sem,
            device_id=target,
            device_id_type=MESH,
        )

    relay_from = (y + 3 + 2 * core) % 4
    relay_to = (y + 1 + 2 * core) % 4
    across_from = (y + 2) % 4

    def arrived(ref, sem):
        pltpu.make_async_copy(ref, ref, sem).wait()

    def to_partner(y_from, kind, step):
        forward(y_from, step, partner, send_c.at[kind], recv_c.at[kind]).start()

    def level0(step):
        arrived(chunk(y, core, (z + 16 - offset_of(step)) % 16, 64), recv_a.at[step])
        forward(y, step, column(up, core), send_y.at[0], recv_y.at[0, step]).start()
        forward(y, step, column(down, core), send_y.at[1], recv_y.at[1, step]).start()
        to_partner(y, 0, step)

        @pl.when(step >= DIRECT)
        def _():
            forward(
                y, step, column(across_from, core), send_y.at[2], recv_y.at[2, step]
            ).start()

        @pl.when(step >= BOTH)
        def _():
            for kind, y_to in ((1, up), (2, down), (3, across_from)):
                forward(
                    y, step, column(y_to, 1 - core), send_c.at[kind], recv_c.at[kind]
                ).start()

    def level1(step):
        forward(down, step, partner, send_y.at[0], recv_y.at[0, step]).wait_recv()
        forward(up, step, partner, send_y.at[1], recv_y.at[1, step]).wait_recv()
        @pl.when(step < DIRECT)
        def _():
            forward(
                relay_from, step, column(relay_to, core), send_y.at[2], recv_y.at[2, step]
            ).start()

        @pl.when(step < BOTH)
        def _():
            to_partner(down, 1, step)
            to_partner(up, 2, step)


    def level2(step):
        forward(across_from, step, partner, send_y.at[2], recv_y.at[2, step]).wait_recv()
        pl.when(step < BOTH)(lambda: to_partner(across_from, 3, step))

    def body(step, carry):
        pl.when(step < 16)(lambda: level0(step))
        pl.when((step >= LAG1) & (step < 16 + LAG1))(lambda: level1(step - LAG1))
        pl.when(step >= LAG2)(lambda: level2(step - LAG2))
        pl.when(step < 8)(lambda: prepare(step))
        pl.when((step >= 8) & (step < 16))(lambda: to_slots(step - 8))
        return carry

    lax.fori_loop(0, 16 + LAG2, body, 0)

    def plane(y_from, core_from):
        return chunk(y_from, core_from, 0, 1024)

    for kind, y_from in enumerate((y, down, up, across_from)):
        arrived(plane(y_from, 1 - core), recv_c.at[kind])

    low_lane = lax.broadcasted_iota(jnp.int32, (128, 128), 1) < 64
    beam_scale = 1.0 / math.sqrt(A)
    mixed = jnp.dot(weight_u[...], x_ref[...], preferred_element_type=jnp.float32)
    for s in range(4):
        sl = slice(s * 128, (s + 1) * 128)
        other = pltpu.roll(mixed[128:256, sl], 64, 1)
        sums = mixed[0:128, sl] + jnp.where(low_lane, -other, other)
        formed_f[pl.ds(s, 128, stride=4), :] = sums * beam_scale
    for e in range(128):
        formed[e] = formed_f[e * 4 : (e + 1) * 4, :].astype(jnp.bfloat16)

    def send_beam(step, turn_by):
        to = ((z + far_offset(step)) % 16) * 8 + (band % 8 + turn_by) % 8
        pltpu.make_async_remote_copy(
            src_ref=formed.at[to],
            dst_ref=beams_ref.at[band],
            send_sem=send_b,
            recv_sem=recv_b,
            device_id=(segment, to),
            device_id_type=MESH,
        ).start()

    def send_beams(step, carry):
        for turn_by in range(8):
            send_beam(step, turn_by)
        return carry

    lax.fori_loop(0, 15, send_beams, 0)
    for turn_by in range(1, 8):
        send_beam(15, turn_by)
    own_beam = pltpu.make_async_copy(formed.at[band], beams_ref.at[band], own_b)
    own_beam.start()

    def reorder(step, carry):
        rows = pl.ds(pl.multiple_of(step * 256, 256), 256)
        ordered[rows, :] = jnp.dot(
            pick[rows, :], x_ref[...], preferred_element_type=jnp.float32
        ).astype(jnp.bfloat16)
        return carry

    lax.fori_loop(0, 8, reorder, 0)

    mine = ordered[pl.ds(pl.multiple_of((half * 4 + segment) * 256, 256), 256), :]
    low_lanes = lax.broadcasted_iota(jnp.int32, (256, 128), 1) < 64
    left[0:256, :] = mine
    for s in range(4):
        sl = slice(s * 128, (s + 1) * 128)
        other = pltpu.roll(mine[:, sl].astype(jnp.float32), 64, 1)
        left[256:512, sl] = jnp.where(low_lanes, other, -other).astype(jnp.bfloat16)
    dims = (((1,), (1,)), ((), ()))

    def correlate(step, carry):
        rows = pl.ds(pl.multiple_of(step * 256, 256), 256)
        gram = lax.dot_general(left[...], ordered[rows, :], dims, preferred_element_type=jnp.float32)
        gram = gram * (1.0 / NB)
        real_ref[:, rows] = gram[0:256]
        imag_ref[:, rows] = gram[256:512]
        return carry

    lax.fori_loop(0, 8, correlate, 0)

    for kind, y_from in enumerate((y, down, up, across_from)):
        arrived(plane(y_from, core), send_c.at[kind])
    for kind in range(3):
        arrived(plane(y, core), send_y.at[kind])
    arrived(spectra.at[pl.ds(0, 63 * 16), :], send_a)
    own_beam.wait()
    arrived(formed.at[pl.ds(0, 127)], send_b)
    arrived(beams_ref.at[pl.ds(0, 127)], recv_b)


def finish_kernel(
    real_ref, imag_ref, beams_ref, high_hbm, low_hbm, real_hbm, imag_hbm, series_hbm,
    high_ref, low_ref, wide, turned, series, out_sem, load,
):
    loads = [
        pltpu.make_async_copy(high_hbm, high_ref, load.at[0]),
        pltpu.make_async_copy(low_hbm, low_ref, load.at[1]),
    ]
    for copy in loads:
        copy.start()
    copies = [
        pltpu.make_async_copy(real_ref, real_hbm.at[0, 0], out_sem.at[0]),
        pltpu.make_async_copy(imag_ref, imag_hbm.at[0, 0], out_sem.at[1]),
    ]
    for copy in copies:
        copy.start()
    for i in range(128):
        wide[i * 4 : (i + 1) * 4, :] = beams_ref[i].astype(jnp.float32)
    for h in range(2):
        for s in range(4):
            block = jnp.transpose(wide[pl.ds(h * 4 + s, 64, stride=8), :])
            for part in range(4):
                turned[h * 128 + s * 32 : h * 128 + (s + 1) * 32, part * 64 : (part + 1) * 64] = block[
                    part * 32 : (part + 1) * 32
                ].astype(jnp.bfloat16)
    for copy in loads:
        copy.wait()
    out = jnp.dot(turned[...], high_ref[...], preferred_element_type=jnp.float32)
    out += jnp.dot(turned[...], low_ref[...], preferred_element_type=jnp.float32)
    for h in range(2):
        for q in range(2):
            series[pl.ds(h * 256 + q, 128, stride=2), :] = out[
                h * 128 : (h + 1) * 128, q * 128 : (q + 1) * 128
            ]
    copies.append(pltpu.make_async_copy(series, series_hbm, out_sem.at[2]))
    copies[2].start()
    for copy in copies:
        copy.wait()


VMEM = pl.BlockSpec(memory_space=pltpu.VMEM)
HBM = pl.BlockSpec(memory_space=pltpu.HBM)


def in_hbm(array):
    return pltpu.with_memory_space_constraint(array, pltpu.HBM)


def per_device(voltages, slot_of_antenna, antenna_positions, beam_directions):
    high, low = forward_tables()
    real, imag, received = pl.pallas_call(
        kernel,
        out_shape=(
            jax.ShapeDtypeStruct((256, A), jnp.float32),
            jax.ShapeDtypeStruct((256, A), jnp.float32),
            jax.ShapeDtypeStruct((128, 4, 128), jnp.bfloat16),
        ),
        in_specs=[HBM] * 7,
        out_specs=(VMEM, VMEM, VMEM),
        scratch_shapes=[
            pltpu.VMEM((2, 16, 4096), jnp.bfloat16),
            pltpu.VMEM((256, 256), jnp.bfloat16),
            pltpu.VMEM((256, 256), jnp.bfloat16),
            pltpu.VMEM((16, 128), jnp.int32),
            pltpu.VMEM((2, A), jnp.int32),
            pltpu.VMEM((2, BEAMS), jnp.int32),
            pltpu.VMEM((1, 128), jnp.float32),
            pltpu.VMEM((2, 512, 128), jnp.float32),
            pltpu.VMEM((512, 256), jnp.bfloat16),
            pltpu.VMEM((1024, 128), jnp.float32),
            pltpu.VMEM((1024, 128), jnp.bfloat16),
            pltpu.VMEM((A, 512), jnp.bfloat16),
            pltpu.VMEM((A, A), jnp.bfloat16),
            pltpu.VMEM((256, A), jnp.bfloat16),
            pltpu.VMEM((256, A), jnp.bfloat16),
            pltpu.VMEM((A, 512), jnp.bfloat16),
            pltpu.VMEM((512, 512), jnp.bfloat16),
            pltpu.VMEM((512, 128), jnp.float32),
            pltpu.VMEM((128, 4, 128), jnp.bfloat16),
            pltpu.SemaphoreType.DMA,
            pltpu.SemaphoreType.DMA((16,)),
            pltpu.SemaphoreType.DMA((3,)),
            pltpu.SemaphoreType.DMA((3, 16)),
            pltpu.SemaphoreType.DMA((4,)),
            pltpu.SemaphoreType.DMA((4,)),
            pltpu.SemaphoreType.DMA,
            pltpu.SemaphoreType.DMA,
            pltpu.SemaphoreType.DMA,
            pltpu.SemaphoreType.DMA((7,)),
            pltpu.SemaphoreType.REGULAR,
            pltpu.SemaphoreType.REGULAR,
        ],
        compiler_params=pltpu.CompilerParams(
            collective_id=0, has_side_effects=True, vmem_limit_bytes=32 * 2**20
        ),
        name="correlator",
    )(
        *(
            in_hbm(array)
            for array in (
                voltages,
                jnp.asarray(high),
                jnp.asarray(low),
                slot_of_antenna.reshape(16, 128),
                antenna_positions.T,
                beam_directions.T,
                jnp.asarray(steering_table()),
            )
        )
    )
    inverse_high, inverse_low = inverse_tables()
    real, imag, series = pl.pallas_call(
        finish_kernel,
        out_shape=(
            jax.ShapeDtypeStruct((1, 1, 256, A), jnp.float32),
            jax.ShapeDtypeStruct((1, 1, 256, A), jnp.float32),
            jax.ShapeDtypeStruct((512, 128), jnp.float32),
        ),
        in_specs=[VMEM] * 3 + [HBM] * 2,
        out_specs=[HBM] * 3,
        scratch_shapes=[
            pltpu.VMEM((256, 256), jnp.bfloat16),
            pltpu.VMEM((256, 256), jnp.bfloat16),
            pltpu.VMEM((512, 128), jnp.float32),
            pltpu.VMEM((256, 256), jnp.bfloat16),
            pltpu.VMEM((512, 128), jnp.float32),
            pltpu.SemaphoreType.DMA((3,)),
            pltpu.SemaphoreType.DMA((2,)),
        ],
        compiler_params=pltpu.CompilerParams(vmem_limit_bytes=16 * 2**20),
        name="finish",
    )(
        real,
        imag,
        received,
        in_hbm(jnp.asarray(inverse_high)),
        in_hbm(jnp.asarray(inverse_low)),
    )
    series = series.reshape(2, 128, 2, 128).transpose(0, 2, 1, 3).reshape(2, 1, 1, 2, NB * 64)
    return (real, imag, series)


def solution(mesh):
    in_specs = (P(None, "band", "segment"), P(), P(), P())
    out_specs = (
        P("band", "segment", None, None),
        P("band", "segment", None, None),
        P(None, "segment", "band", None, None),
    )
    return jax.shard_map(
        per_device, mesh=mesh, in_specs=in_specs, out_specs=out_specs, check_vma=False
    )
```

```python
import math

import jax
import jax.numpy as jnp
import numpy as np
from jax import lax
from jax.experimental import pallas as pl
from jax.experimental.pallas import tpu as pltpu
from jax.sharding import PartitionSpec as P

A = 2048
C = 64
BEAMS = 1024
NB = 256
MESH = pl.DeviceIdType.MESH
LAG1 = 8
LAG2 = 8
NEAR = 6
FAR = 2 * NEAR + 1
DIRECT = 0
BOTH = 14


def dft_parts():
    index = np.arange(64)
    theta = (np.outer(index, index) % 64) * (2.0 * math.pi / 64.0)
    return np.cos(theta) * 0.125, np.sin(theta) * 0.125


def split(table):
    high = table.astype(np.float32).astype(jnp.bfloat16)
    low = (table - high.astype(np.float64)).astype(np.float32).astype(jnp.bfloat16)
    return high, low


def forward_tables():
    cosine, sine = dft_parts()
    parts = np.array([[cosine, -sine], [sine, cosine]])
    table = np.zeros((2, 2, 64, 2, 2, 64))
    for t1 in range(2):
        table[:, t1, :, :, t1, :] = parts.transpose(1, 3, 0, 2)
    return split(table.reshape(256, 256))


def inverse_tables():
    cosine, sine = dft_parts()
    parts = np.array([[cosine, sine], [-sine, cosine]])
    table = np.zeros((2, 2, 64, 2, 2, 64))
    for t1 in range(2):
        table[:, t1, :, :, t1, :] = parts.transpose(0, 2, 1, 3)
    return split(table.reshape(256, 256))


def steering_table():
    phase = np.arange(64) * (2.0 * math.pi / 64.0)
    row = np.concatenate([np.cos(phase), -np.sin(phase)]).astype(np.float32)
    return row.reshape(1, 128)


def place():
    segment = lax.axis_index("segment")
    band = lax.axis_index("band")
    core, half, channel = segment % 2, band % 2, band // 2
    return segment, band, core, half, channel, channel // 4, channel % 4, half * 2 + segment // 2


def near_offset(step):
    odd = step % 2
    return (odd * ((step + 1) // 2) + (1 - odd) * (16 - step // 2)) % 16


def far_offset(step):
    odd = step % 2
    return (8 - odd * ((step + 1) // 2) + (1 - odd) * (step // 2)) % 16


def offset_of(step):
    return jnp.where(step < FAR, near_offset(step), far_offset(jnp.maximum(step - FAR, 0)))


def channelize(v_ref, high_ref, low_ref, wide, turned, spectra_f, spectra):
    for p in range(2):
        for t2 in range(32):
            wide[p, t2 * 16 : (t2 + 1) * 16, :] = v_ref[p, :, t2 * 128 : (t2 + 1) * 128].astype(
                jnp.float32
            )
    for a in range(16):
        for p in range(2):
            turned[a * 32 : (a + 1) * 32, p * 128 : (p + 1) * 128] = wide[
                p, pl.ds(a, 32, stride=16), :
            ].astype(jnp.bfloat16)
    dims = (((1,), (1,)), ((), ()))
    lane = lax.broadcasted_iota(jnp.int32, (64, 128), 1)
    first, even = lane < 64, (lane // 32) % 2 == 0
    for g in range(4):
        block = turned[g * 128 : (g + 1) * 128, :]
        out = lax.dot_general(high_ref[...], block, dims, preferred_element_type=jnp.float32)
        out += lax.dot_general(low_ref[...], block, dims, preferred_element_type=jnp.float32)
        part = [out[i * 64 : (i + 1) * 64] for i in range(4)]
        for i in range(2):
            a, b = part[i], part[i + 2]
            part[i] = jnp.where(first, a, pltpu.roll(b, 64, 1))
            part[i + 2] = jnp.where(first, pltpu.roll(a, 64, 1), b)
        for i in (0, 2):
            a, b = part[i], part[i + 1]
            part[i] = jnp.where(even, a, pltpu.roll(b, 32, 1))
            part[i + 1] = jnp.where(even, pltpu.roll(a, 96, 1), b)
        for i in range(4):
            spectra_f[pl.ds(g * 4 + i, 64, stride=16), :] = part[i]
    spectra[...] = spectra_f[...].astype(jnp.bfloat16)


def column_of(row):
    return jnp.transpose(jnp.broadcast_to(row, (128, 128)))


def build_pick(slot_ref, pick, r):
    lane = lax.broadcasted_iota(jnp.int32, (128, 128), 1)
    slot = column_of(slot_ref[pl.ds(r, 1), :])
    rows = pl.ds(pl.multiple_of(r * 128, 128), 128)
    for c in range(16):
        position = lane + c * 128
        name = ((position % 1024) // 16) * 32 + (position // 1024) * 16 + position % 16
        pick[rows, c * 128 : (c + 1) * 128] = jnp.where(slot == name, 1.0, 0.0).astype(jnp.bfloat16)


def build_weights(pos_ref, turn, tab_ref, weight_a, c):
    table = jnp.broadcast_to(tab_ref[...], (128, 128))
    lanes = pl.ds(pl.multiple_of(c * 128, 128), 128)
    phase = (turn[0] * pos_ref[0:1, lanes] + turn[1] * pos_ref[1:2, lanes]) & 63
    weight_a[0:128, lanes] = jnp.take_along_axis(table, phase, axis=1).astype(jnp.bfloat16)
    weight_a[128:256, lanes] = jnp.take_along_axis(table, phase + 64, axis=1).astype(jnp.bfloat16)


def kernel(
    v_hbm, high_hbm, low_hbm, slot_hbm, pos_hbm, dir_hbm, tab_hbm,
    real_ref, imag_ref, beams_ref,
    v_ref, high_ref, low_ref, slot_ref, pos_ref, dir_ref, tab_ref,
    wide, turned, spectra_f, spectra, x_ref, pick, weight_a, weight_u, ordered, left,
    formed_f, formed,
    send_a, recv_a, send_y, recv_y, send_c, recv_c, send_b, recv_b, own_b, load, from_above, from_below,
):
    segment, band, core, half, channel, z, x, y = place()
    loads = [
        pltpu.make_async_copy(source, target, load.at[i])
        for i, (source, target) in enumerate(
            (
                (v_hbm, v_ref),
                (high_hbm, high_ref),
                (low_hbm, low_ref),
                (slot_hbm, slot_ref),
                (pos_hbm, pos_ref),
                (dir_hbm, dir_ref),
                (tab_hbm, tab_ref),
            )
        )
    ]
    for copy in loads:
        copy.start()

    def column(y_to, core_to):
        return ((y_to % 2) * 2 + core_to, channel * 2 + y_to // 2)

    up, down = (y + 1) % 4, (y + 3) % 4
    partner = column(y, 1 - core)
    barrier = pltpu.get_barrier_semaphore()

    above, below = ((z + 1) % 16) * 4 + x, ((z + 15) % 16) * 4 + x

    def beside(other):
        return (segment, other * 2 + half)

    greeted = [beside(z * 4 + (x + across) % 4) for across in range(1, 4)]
    greeted += [beside(above), beside(below), column(up, core), column(down, core), partner]
    greeted += [column((y + 2) % 4, core), column((y + 2) % 4, 1 - core)]
    greeted += [column(up, 1 - core), column(down, 1 - core)]
    for target in greeted:
        pl.semaphore_signal(barrier, inc=1, device_id=target, device_id_type=MESH)

    for copy in loads:
        copy.wait()
    channelize(v_ref, high_ref, low_ref, wide, turned, spectra_f, spectra)
    pl.semaphore_wait(barrier, 12)

    def tell(sem, target):
        pl.semaphore_signal(sem, inc=1, device_id=beside(target), device_id_type=MESH)

    tell(from_above, below)
    tell(from_below, above)

    def chunk(y_from, core_from, z_from, rows):
        row = pl.multiple_of((y_from // 2) * 1024 + z_from * 64, 64)
        lane = pl.multiple_of(((y_from % 2) * 2 + core_from) * 128, 128)
        return x_ref.at[pl.ds(row, rows), pl.ds(lane, 128)]

    home = x_ref.at[
        pl.ds(pl.multiple_of(half * 1024 + channel * 16, 16), 16),
        pl.ds(pl.multiple_of(segment * 128, 128), 128),
    ]

    columns = [(x + across) % 4 for across in range(4)]

    def message(step, across, base):
        to = base + columns[across]
        return pltpu.make_async_remote_copy(
            src_ref=spectra.at[pl.ds(pl.multiple_of(to * 16, 16), 16), :],
            dst_ref=home,
            send_sem=send_a,
            recv_sem=recv_a.at[step],
            device_id=(segment, to * 2 + half),
            device_id_type=MESH,
        )

    own = pltpu.make_async_copy(
        spectra.at[pl.ds(pl.multiple_of(channel * 16, 16), 16), :], home, recv_a.at[0]
    )
    own.start()
    for across in range(1, 4):
        message(0, across, z * 4).start()

    def messages(step):
        base = ((z + offset_of(step)) % 16) * 4
        for across in range(4):
            message(step, across, base).start()

    start = pl.multiple_of(half * 512 + segment * 128, 128)
    turn = [column_of(dir_ref[i : i + 1, pl.ds(start, 128)]) * channel for i in range(2)]

    def reach(d, carry):
        pl.semaphore_wait(from_above, 1)
        tell(from_above, below)
        pl.semaphore_wait(from_below, 1)
        pl.when(d < 7)(lambda: tell(from_below, above))

        @pl.when(d <= NEAR)
        def _():
            messages(2 * d - 1)
            messages(2 * d)

        return carry

    lax.fori_loop(1, 8, reach, 0)
    pl.semaphore_wait(from_above, 1)

    def send_far(step, carry):
        messages(step)
        return carry

    lax.fori_loop(FAR, 16, send_far, 0)

    def prepare(step):
        for i in range(2):
            build_pick(slot_ref, pick, 2 * step + i)
            build_weights(pos_ref, turn, tab_ref, weight_a, 2 * step + i)

    def to_slots(c):
        lanes = pl.ds(pl.multiple_of(c * 256, 256), 256)
        weight_u[:, lanes] = jnp.dot(
            weight_a[...], pick[:, lanes], preferred_element_type=jnp.float32
        ).astype(jnp.bfloat16)

    def forward(y_from, step, target, send_sem, recv_sem):
        source = chunk(y_from, core, (z + 16 - offset_of(step)) % 16, 64)
        return pltpu.make_async_remote_copy(
            src_ref=source,
            dst_ref=source,
            send_sem=send_sem,
            recv_sem=recv_sem,
            device_id=target,
            device_id_type=MESH,
        )

    relay_from = (y + 3 + 2 * core) % 4
    relay_to = (y + 1 + 2 * core) % 4
    across_from = (y + 2) % 4

    def arrived(ref, sem):
        pltpu.make_async_copy(ref, ref, sem).wait()

    def to_partner(y_from, kind, step):
        forward(y_from, step, partner, send_c.at[kind], recv_c.at[kind]).start()

    def level0(step):
        arrived(chunk(y, core, (z + 16 - offset_of(step)) % 16, 64), recv_a.at[step])
        forward(y, step, column(up, core), send_y.at[0], recv_y.at[0, step]).start()
        forward(y, step, column(down, core), send_y.at[1], recv_y.at[1, step]).start()
        to_partner(y, 0, step)

        @pl.when(step >= DIRECT)
        def _():
            forward(
                y, step, column(across_from, core), send_y.at[2], recv_y.at[2, step]
            ).start()

        @pl.when(step >= BOTH)
        def _():
            for kind, y_to in ((1, up), (2, down), (3, across_from)):
                forward(
                    y, step, column(y_to, 1 - core), send_c.at[kind], recv_c.at[kind]
                ).start()

    def level1(step):
        forward(down, step, partner, send_y.at[0], recv_y.at[0, step]).wait_recv()
        forward(up, step, partner, send_y.at[1], recv_y.at[1, step]).wait_recv()
        @pl.when(step < DIRECT)
        def _():
            forward(
                relay_from, step, column(relay_to, core), send_y.at[2], recv_y.at[2, step]
            ).start()

        @pl.when(step < BOTH)
        def _():
            to_partner(down, 1, step)
            to_partner(up, 2, step)


    def level2(step):
        forward(across_from, step, partner, send_y.at[2], recv_y.at[2, step]).wait_recv()
        pl.when(step < BOTH)(lambda: to_partner(across_from, 3, step))

    def body(step, carry):
        pl.when(step < 16)(lambda: level0(step))
        pl.when((step >= LAG1) & (step < 16 + LAG1))(lambda: level1(step - LAG1))
        pl.when(step >= LAG2)(lambda: level2(step - LAG2))
        pl.when(step < 8)(lambda: prepare(step))
        pl.when((step >= 8) & (step < 16))(lambda: to_slots(step - 8))
        return carry

    lax.fori_loop(0, 16 + LAG2, body, 0)

    def plane(y_from, core_from):
        return chunk(y_from, core_from, 0, 1024)

    for kind, y_from in enumerate((y, down, up, across_from)):
        arrived(plane(y_from, 1 - core), recv_c.at[kind])

    low_lane = lax.broadcasted_iota(jnp.int32, (128, 128), 1) < 64
    beam_scale = 1.0 / math.sqrt(A)
    mixed = jnp.dot(weight_u[...], x_ref[...], preferred_element_type=jnp.float32)
    for s in range(4):
        sl = slice(s * 128, (s + 1) * 128)
        other = pltpu.roll(mixed[128:256, sl], 64, 1)
        sums = mixed[0:128, sl] + jnp.where(low_lane, -other, other)
        formed_f[pl.ds(s, 128, stride=4), :] = sums * beam_scale
    for e in range(128):
        formed[e] = formed_f[e * 4 : (e + 1) * 4, :].astype(jnp.bfloat16)

    lows = [(band % 8 + turn_by) % 8 for turn_by in range(8)]

    def send_beam(to):
        pltpu.make_async_remote_copy(
            src_ref=formed.at[to],
            dst_ref=beams_ref.at[band],
            send_sem=send_b,
            recv_sem=recv_b,
            device_id=(segment, to),
            device_id_type=MESH,
        ).start()

    def send_beams(step, carry):
        base = ((z + far_offset(step)) % 16) * 8
        for low in lows:
            send_beam(base + low)
        return carry

    lax.fori_loop(0, 15, send_beams, 0)
    for low in lows[1:]:
        send_beam(z * 8 + low)
    own_beam = pltpu.make_async_copy(formed.at[band], beams_ref.at[band], own_b)
    own_beam.start()

    def reorder(step, carry):
        rows = pl.ds(pl.multiple_of(step * 256, 256), 256)
        ordered[rows, :] = jnp.dot(
            pick[rows, :], x_ref[...], preferred_element_type=jnp.float32
        ).astype(jnp.bfloat16)
        return carry

    lax.fori_loop(0, 8, reorder, 0)

    mine = ordered[pl.ds(pl.multiple_of((half * 4 + segment) * 256, 256), 256), :]
    low_lanes = lax.broadcasted_iota(jnp.int32, (256, 128), 1) < 64
    left[0:256, :] = mine
    for s in range(4):
        sl = slice(s * 128, (s + 1) * 128)
        other = pltpu.roll(mine[:, sl].astype(jnp.float32), 64, 1)
        left[256:512, sl] = jnp.where(low_lanes, other, -other).astype(jnp.bfloat16)
    dims = (((1,), (1,)), ((), ()))

    def correlate(step, carry):
        rows = pl.ds(pl.multiple_of(step * 256, 256), 256)
        gram = lax.dot_general(left[...], ordered[rows, :], dims, preferred_element_type=jnp.float32)
        gram = gram * (1.0 / NB)
        real_ref[:, rows] = gram[0:256]
        imag_ref[:, rows] = gram[256:512]
        return carry

    lax.fori_loop(0, 8, correlate, 0)

    for kind, y_from in enumerate((y, down, up, across_from)):
        arrived(plane(y_from, core), send_c.at[kind])
    for kind in range(3):
        arrived(plane(y, core), send_y.at[kind])
    arrived(spectra.at[pl.ds(0, 63 * 16), :], send_a)
    own_beam.wait()
    arrived(formed.at[pl.ds(0, 127)], send_b)
    arrived(beams_ref.at[pl.ds(0, 127)], recv_b)


def finish_kernel(
    real_ref, imag_ref, beams_ref, high_hbm, low_hbm, real_hbm, imag_hbm, series_hbm,
    high_ref, low_ref, wide, turned, series, out_sem, load,
):
    loads = [
        pltpu.make_async_copy(high_hbm, high_ref, load.at[0]),
        pltpu.make_async_copy(low_hbm, low_ref, load.at[1]),
    ]
    for copy in loads:
        copy.start()
    copies = [
        pltpu.make_async_copy(real_ref, real_hbm.at[0, 0], out_sem.at[0]),
        pltpu.make_async_copy(imag_ref, imag_hbm.at[0, 0], out_sem.at[1]),
    ]
    for copy in copies:
        copy.start()
    for i in range(128):
        wide[i * 4 : (i + 1) * 4, :] = beams_ref[i].astype(jnp.float32)
    for h in range(2):
        for s in range(4):
            block = jnp.transpose(wide[pl.ds(h * 4 + s, 64, stride=8), :])
            for part in range(4):
                turned[h * 128 + s * 32 : h * 128 + (s + 1) * 32, part * 64 : (part + 1) * 64] = block[
                    part * 32 : (part + 1) * 32
                ].astype(jnp.bfloat16)
    for copy in loads:
        copy.wait()
    out = jnp.dot(turned[...], high_ref[...], preferred_element_type=jnp.float32)
    out += jnp.dot(turned[...], low_ref[...], preferred_element_type=jnp.float32)
    for h in range(2):
        for q in range(2):
            series[pl.ds(h * 256 + q, 128, stride=2), :] = out[
                h * 128 : (h + 1) * 128, q * 128 : (q + 1) * 128
            ]
    copies.append(pltpu.make_async_copy(series, series_hbm, out_sem.at[2]))
    copies[2].start()
    for copy in copies:
        copy.wait()


VMEM = pl.BlockSpec(memory_space=pltpu.VMEM)
HBM = pl.BlockSpec(memory_space=pltpu.HBM)


def in_hbm(array):
    return pltpu.with_memory_space_constraint(array, pltpu.HBM)


def per_device(voltages, slot_of_antenna, antenna_positions, beam_directions):
    high, low = forward_tables()
    real, imag, received = pl.pallas_call(
        kernel,
        out_shape=(
            jax.ShapeDtypeStruct((256, A), jnp.float32),
            jax.ShapeDtypeStruct((256, A), jnp.float32),
            jax.ShapeDtypeStruct((128, 4, 128), jnp.bfloat16),
        ),
        in_specs=[HBM] * 7,
        out_specs=(VMEM, VMEM, VMEM),
        scratch_shapes=[
            pltpu.VMEM((2, 16, 4096), jnp.bfloat16),
            pltpu.VMEM((256, 256), jnp.bfloat16),
            pltpu.VMEM((256, 256), jnp.bfloat16),
            pltpu.VMEM((16, 128), jnp.int32),
            pltpu.VMEM((2, A), jnp.int32),
            pltpu.VMEM((2, BEAMS), jnp.int32),
            pltpu.VMEM((1, 128), jnp.float32),
            pltpu.VMEM((2, 512, 128), jnp.float32),
            pltpu.VMEM((512, 256), jnp.bfloat16),
            pltpu.VMEM((1024, 128), jnp.float32),
            pltpu.VMEM((1024, 128), jnp.bfloat16),
            pltpu.VMEM((A, 512), jnp.bfloat16),
            pltpu.VMEM((A, A), jnp.bfloat16),
            pltpu.VMEM((256, A), jnp.bfloat16),
            pltpu.VMEM((256, A), jnp.bfloat16),
            pltpu.VMEM((A, 512), jnp.bfloat16),
            pltpu.VMEM((512, 512), jnp.bfloat16),
            pltpu.VMEM((512, 128), jnp.float32),
            pltpu.VMEM((128, 4, 128), jnp.bfloat16),
            pltpu.SemaphoreType.DMA,
            pltpu.SemaphoreType.DMA((16,)),
            pltpu.SemaphoreType.DMA((3,)),
            pltpu.SemaphoreType.DMA((3, 16)),
            pltpu.SemaphoreType.DMA((4,)),
            pltpu.SemaphoreType.DMA((4,)),
            pltpu.SemaphoreType.DMA,
            pltpu.SemaphoreType.DMA,
            pltpu.SemaphoreType.DMA,
            pltpu.SemaphoreType.DMA((7,)),
            pltpu.SemaphoreType.REGULAR,
            pltpu.SemaphoreType.REGULAR,
        ],
        compiler_params=pltpu.CompilerParams(
            collective_id=0, has_side_effects=True, vmem_limit_bytes=32 * 2**20
        ),
        name="correlator",
    )(
        *(
            in_hbm(array)
            for array in (
                voltages,
                jnp.asarray(high),
                jnp.asarray(low),
                slot_of_antenna.reshape(16, 128),
                antenna_positions.T,
                beam_directions.T,
                jnp.asarray(steering_table()),
            )
        )
    )
    inverse_high, inverse_low = inverse_tables()
    real, imag, series = pl.pallas_call(
        finish_kernel,
        out_shape=(
            jax.ShapeDtypeStruct((1, 1, 256, A), jnp.float32),
            jax.ShapeDtypeStruct((1, 1, 256, A), jnp.float32),
            jax.ShapeDtypeStruct((512, 128), jnp.float32),
        ),
        in_specs=[VMEM] * 3 + [HBM] * 2,
        out_specs=[HBM] * 3,
        scratch_shapes=[
            pltpu.VMEM((256, 256), jnp.bfloat16),
            pltpu.VMEM((256, 256), jnp.bfloat16),
            pltpu.VMEM((512, 128), jnp.float32),
            pltpu.VMEM((256, 256), jnp.bfloat16),
            pltpu.VMEM((512, 128), jnp.float32),
            pltpu.SemaphoreType.DMA((3,)),
            pltpu.SemaphoreType.DMA((2,)),
        ],
        compiler_params=pltpu.CompilerParams(vmem_limit_bytes=16 * 2**20),
        name="finish",
    )(
        real,
        imag,
        received,
        in_hbm(jnp.asarray(inverse_high)),
        in_hbm(jnp.asarray(inverse_low)),
    )
    series = series.reshape(2, 128, 2, 128).transpose(0, 2, 1, 3).reshape(2, 1, 1, 2, NB * 64)
    return (real, imag, series)


def solution(mesh):
    in_specs = (P(None, "band", "segment"), P(), P(), P())
    out_specs = (
        P("band", "segment", None, None),
        P("band", "segment", None, None),
        P(None, "segment", "band", None, None),
    )
    return jax.shard_map(
        per_device, mesh=mesh, in_specs=in_specs, out_specs=out_specs, check_vma=False
    )
```

```python
import math

import jax
import jax.numpy as jnp
import numpy as np
from jax import lax
from jax.experimental import pallas as pl
from jax.experimental.pallas import tpu as pltpu
from jax.sharding import PartitionSpec as P

A = 2048
C = 64
BEAMS = 1024
NB = 256
MESH = pl.DeviceIdType.MESH
LAG1 = 8
LAG2 = 8
NEAR = 6
FAR = 2 * NEAR + 1
DIRECT = 0
BOTH = 14


def dft_parts():
    index = np.arange(64)
    theta = (np.outer(index, index) % 64) * (2.0 * math.pi / 64.0)
    return np.cos(theta) * 0.125, np.sin(theta) * 0.125


def split(table):
    high = table.astype(np.float32).astype(jnp.bfloat16)
    low = (table - high.astype(np.float64)).astype(np.float32).astype(jnp.bfloat16)
    return high, low


def forward_tables():
    cosine, sine = dft_parts()
    parts = np.array([[cosine, -sine], [sine, cosine]])
    table = np.zeros((2, 2, 64, 2, 2, 64))
    for t1 in range(2):
        table[:, t1, :, :, t1, :] = parts.transpose(1, 3, 0, 2)
    return split(table.reshape(256, 256))


def inverse_tables():
    cosine, sine = dft_parts()
    parts = np.array([[cosine, sine], [-sine, cosine]])
    table = np.zeros((2, 2, 64, 2, 2, 64))
    for t1 in range(2):
        table[:, t1, :, :, t1, :] = parts.transpose(0, 2, 1, 3)
    return split(table.reshape(256, 256))


def steering_table():
    phase = np.arange(64) * (2.0 * math.pi / 64.0)
    row = np.concatenate([np.cos(phase), -np.sin(phase)]).astype(np.float32)
    return row.reshape(1, 128)


def place():
    segment = lax.axis_index("segment")
    band = lax.axis_index("band")
    core, half, channel = segment % 2, band % 2, band // 2
    return segment, band, core, half, channel, channel // 4, channel % 4, half * 2 + segment // 2


def near_offset(step):
    odd = step % 2
    return (odd * ((step + 1) // 2) + (1 - odd) * (16 - step // 2)) % 16


def far_offset(step):
    odd = step % 2
    return (8 - odd * ((step + 1) // 2) + (1 - odd) * (step // 2)) % 16


def offset_of(step):
    return jnp.where(step < FAR, near_offset(step), far_offset(jnp.maximum(step - FAR, 0)))


def channelize(v_ref, high_ref, low_ref, wide, turned, spectra_f, spectra):
    for p in range(2):
        for t2 in range(32):
            wide[p, t2 * 16 : (t2 + 1) * 16, :] = v_ref[p, :, t2 * 128 : (t2 + 1) * 128].astype(
                jnp.float32
            )
    for a in range(16):
        for p in range(2):
            turned[a * 32 : (a + 1) * 32, p * 128 : (p + 1) * 128] = wide[
                p, pl.ds(a, 32, stride=16), :
            ].astype(jnp.bfloat16)
    dims = (((1,), (1,)), ((), ()))
    lane = lax.broadcasted_iota(jnp.int32, (64, 128), 1)
    first, even = lane < 64, (lane // 32) % 2 == 0
    for g in range(4):
        block = turned[g * 128 : (g + 1) * 128, :]
        out = lax.dot_general(high_ref[...], block, dims, preferred_element_type=jnp.float32)
        out += lax.dot_general(low_ref[...], block, dims, preferred_element_type=jnp.float32)
        part = [out[i * 64 : (i + 1) * 64] for i in range(4)]
        for i in range(2):
            a, b = part[i], part[i + 2]
            part[i] = jnp.where(first, a, pltpu.roll(b, 64, 1))
            part[i + 2] = jnp.where(first, pltpu.roll(a, 64, 1), b)
        for i in (0, 2):
            a, b = part[i], part[i + 1]
            part[i] = jnp.where(even, a, pltpu.roll(b, 32, 1))
            part[i + 1] = jnp.where(even, pltpu.roll(a, 96, 1), b)
        for i in range(4):
            spectra_f[pl.ds(g * 4 + i, 64, stride=16), :] = part[i]
    spectra[...] = spectra_f[...].astype(jnp.bfloat16)


def column_of(row):
    return jnp.transpose(jnp.broadcast_to(row, (128, 128)))


def build_pick(slot_ref, pick, r):
    lane = lax.broadcasted_iota(jnp.int32, (128, 128), 1)
    slot = column_of(slot_ref[pl.ds(r, 1), :])
    rows = pl.ds(pl.multiple_of(r * 128, 128), 128)
    for c in range(16):
        position = lane + c * 128
        name = ((position % 1024) // 16) * 32 + (position // 1024) * 16 + position % 16
        pick[rows, c * 128 : (c + 1) * 128] = jnp.where(slot == name, 1.0, 0.0).astype(jnp.bfloat16)


def build_weights(pos_ref, turn, tab_ref, weight_a, c):
    table = jnp.broadcast_to(tab_ref[...], (128, 128))
    lanes = pl.ds(pl.multiple_of(c * 128, 128), 128)
    phase = (turn[0] * pos_ref[0:1, lanes] + turn[1] * pos_ref[1:2, lanes]) & 63
    weight_a[0:128, lanes] = jnp.take_along_axis(table, phase, axis=1).astype(jnp.bfloat16)
    weight_a[128:256, lanes] = jnp.take_along_axis(table, phase + 64, axis=1).astype(jnp.bfloat16)


def kernel(
    v_hbm, high_hbm, low_hbm, slot_hbm, pos_hbm, dir_hbm, tab_hbm,
    real_ref, imag_ref, beams_ref,
    v_ref, high_ref, low_ref, slot_ref, pos_ref, dir_ref, tab_ref,
    wide, turned, spectra_f, spectra, x_ref, pick, weight_a, weight_u, ordered, left,
    formed_f, formed,
    send_a, recv_a, send_y, recv_y, send_c, recv_c, send_b, recv_b, own_b, load, from_above, from_below,
):
    segment, band, core, half, channel, z, x, y = place()
    loads = [
        pltpu.make_async_copy(source, target, load.at[i])
        for i, (source, target) in enumerate(
            (
                (v_hbm, v_ref),
                (high_hbm, high_ref),
                (low_hbm, low_ref),
                (slot_hbm, slot_ref),
                (pos_hbm, pos_ref),
                (dir_hbm, dir_ref),
                (tab_hbm, tab_ref),
            )
        )
    ]
    for copy in loads:
        copy.start()

    def column(y_to, core_to):
        return ((y_to % 2) * 2 + core_to, channel * 2 + y_to // 2)

    up, down = (y + 1) % 4, (y + 3) % 4
    partner = column(y, 1 - core)
    barrier = pltpu.get_barrier_semaphore()

    above, below = ((z + 1) % 16) * 4 + x, ((z + 15) % 16) * 4 + x

    def beside(other):
        return (segment, other * 2 + half)

    greeted = [beside(z * 4 + (x + across) % 4) for across in range(1, 4)]
    greeted += [beside(above), beside(below), column(up, core), column(down, core), partner]
    greeted += [column((y + 2) % 4, core), column((y + 2) % 4, 1 - core)]
    greeted += [column(up, 1 - core), column(down, 1 - core)]
    for target in greeted:
        pl.semaphore_signal(barrier, inc=1, device_id=target, device_id_type=MESH)

    for copy in loads:
        copy.wait()
    channelize(v_ref, high_ref, low_ref, wide, turned, spectra_f, spectra)
    pl.semaphore_wait(barrier, 12)

    def tell(sem, target):
        pl.semaphore_signal(sem, inc=1, device_id=beside(target), device_id_type=MESH)

    tell(from_above, below)
    tell(from_below, above)

    def chunk(y_from, core_from, z_from, rows):
        row = pl.multiple_of((y_from // 2) * 1024 + z_from * 64, 64)
        lane = pl.multiple_of(((y_from % 2) * 2 + core_from) * 128, 128)
        return x_ref.at[pl.ds(row, rows), pl.ds(lane, 128)]

    home = x_ref.at[
        pl.ds(pl.multiple_of(half * 1024 + channel * 16, 16), 16),
        pl.ds(pl.multiple_of(segment * 128, 128), 128),
    ]

    columns = [(x + across) % 4 for across in range(4)]

    def message(step, across, base):
        to = base + columns[across]
        return pltpu.make_async_remote_copy(
            src_ref=spectra.at[pl.ds(pl.multiple_of(to * 16, 16), 16), :],
            dst_ref=home,
            send_sem=send_a,
            recv_sem=recv_a.at[step],
            device_id=(segment, to * 2 + half),
            device_id_type=MESH,
        )

    own = pltpu.make_async_copy(
        spectra.at[pl.ds(pl.multiple_of(channel * 16, 16), 16), :], home, recv_a.at[0]
    )
    own.start()
    for across in range(1, 4):
        message(0, across, z * 4).start()

    def messages(step):
        base = ((z + offset_of(step)) % 16) * 4
        for across in range(4):
            message(step, across, base).start()

    start = pl.multiple_of(half * 512 + segment * 128, 128)
    turn = [column_of(dir_ref[i : i + 1, pl.ds(start, 128)]) * channel for i in range(2)]

    def reach(d, carry):
        pl.semaphore_wait(from_above, 1)
        tell(from_above, below)
        pl.semaphore_wait(from_below, 1)
        pl.when(d < 7)(lambda: tell(from_below, above))

        @pl.when(d <= NEAR)
        def _():
            messages(2 * d - 1)
            messages(2 * d)

        return carry

    lax.fori_loop(1, 8, reach, 0)
    pl.semaphore_wait(from_above, 1)

    def send_far(step, carry):
        messages(step)
        return carry

    lax.fori_loop(FAR, 16, send_far, 0)

    def prepare(step):
        for i in range(2):
            build_pick(slot_ref, pick, 2 * step + i)
            build_weights(pos_ref, turn, tab_ref, weight_a, 2 * step + i)

    def to_slots(c):
        lanes = pl.ds(pl.multiple_of(c * 256, 256), 256)
        weight_u[:, lanes] = jnp.dot(
            weight_a[...], pick[:, lanes], preferred_element_type=jnp.float32
        ).astype(jnp.bfloat16)

    def forward(y_from, step, target, send_sem, recv_sem):
        source = chunk(y_from, core, (z + 16 - offset_of(step)) % 16, 64)
        return pltpu.make_async_remote_copy(
            src_ref=source,
            dst_ref=source,
            send_sem=send_sem,
            recv_sem=recv_sem,
            device_id=target,
            device_id_type=MESH,
        )

    relay_from = (y + 3 + 2 * core) % 4
    relay_to = (y + 1 + 2 * core) % 4
    across_from = (y + 2) % 4

    def arrived(ref, sem):
        pltpu.make_async_copy(ref, ref, sem).wait()

    def to_partner(y_from, kind, step):
        forward(y_from, step, partner, send_c.at[kind], recv_c.at[kind]).start()

    def level0(step):
        arrived(chunk(y, core, (z + 16 - offset_of(step)) % 16, 64), recv_a.at[step])
        forward(y, step, column(up, core), send_y.at[0], recv_y.at[0, step]).start()
        forward(y, step, column(down, core), send_y.at[1], recv_y.at[1, step]).start()
        to_partner(y, 0, step)

        @pl.when(step >= DIRECT)
        def _():
            forward(
                y, step, column(across_from, core), send_y.at[2], recv_y.at[2, step]
            ).start()

        @pl.when(step >= BOTH)
        def _():
            for kind, y_to in ((1, up), (2, down), (3, across_from)):
                forward(
                    y, step, column(y_to, 1 - core), send_c.at[kind], recv_c.at[kind]
                ).start()

    def level1(step):
        forward(down, step, partner, send_y.at[0], recv_y.at[0, step]).wait_recv()
        forward(up, step, partner, send_y.at[1], recv_y.at[1, step]).wait_recv()
        @pl.when(step < DIRECT)
        def _():
            forward(
                relay_from, step, column(relay_to, core), send_y.at[2], recv_y.at[2, step]
            ).start()

        @pl.when(step < BOTH)
        def _():
            to_partner(down, 1, step)
            to_partner(up, 2, step)


    def level2(step):
        forward(across_from, step, partner, send_y.at[2], recv_y.at[2, step]).wait_recv()
        pl.when(step < BOTH)(lambda: to_partner(across_from, 3, step))

    def body(step, carry):
        pl.when(step < 16)(lambda: level0(step))
        pl.when((step >= LAG1) & (step < 16 + LAG1))(lambda: level1(step - LAG1))
        pl.when(step >= LAG2)(lambda: level2(step - LAG2))
        pl.when(step < 8)(lambda: prepare(step))
        pl.when((step >= 8) & (step < 16))(lambda: to_slots(step - 8))
        return carry

    lax.fori_loop(0, 16 + LAG2, body, 0)

    def plane(y_from, core_from):
        return chunk(y_from, core_from, 0, 1024)

    for kind, y_from in enumerate((y, down, up, across_from)):
        arrived(plane(y_from, 1 - core), recv_c.at[kind])

    low_lane = lax.broadcasted_iota(jnp.int32, (128, 128), 1) < 64
    beam_scale = 1.0 / math.sqrt(A)
    mixed = jnp.dot(weight_u[...], x_ref[...], preferred_element_type=jnp.float32)
    for s in range(4):
        sl = slice(s * 128, (s + 1) * 128)
        other = pltpu.roll(mixed[128:256, sl], 64, 1)
        sums = mixed[0:128, sl] + jnp.where(low_lane, -other, other)
        formed_f[pl.ds(s, 128, stride=4), :] = sums * beam_scale
    for e in range(128):
        formed[e] = formed_f[e * 4 : (e + 1) * 4, :].astype(jnp.bfloat16)

    lows = [(band % 8 + turn_by) % 8 for turn_by in range(8)]

    def send_beam(to):
        pltpu.make_async_remote_copy(
            src_ref=formed.at[to],
            dst_ref=beams_ref.at[band],
            send_sem=send_b,
            recv_sem=recv_b,
            device_id=(segment, to),
            device_id_type=MESH,
        ).start()

    def send_beams(step, carry):
        base = ((z + far_offset(step)) % 16) * 8
        for low in lows:
            send_beam(base + low)
        return carry

    lax.fori_loop(0, 15, send_beams, 0)
    for low in lows[1:]:
        send_beam(z * 8 + low)
    own_beam = pltpu.make_async_copy(formed.at[band], beams_ref.at[band], own_b)
    own_beam.start()

    def reorder(step, carry):
        rows = pl.ds(pl.multiple_of(step * 256, 256), 256)
        ordered[rows, :] = jnp.dot(
            pick[rows, :], x_ref[...], preferred_element_type=jnp.float32
        ).astype(jnp.bfloat16)
        return carry

    lax.fori_loop(0, 8, reorder, 0)

    mine = ordered[pl.ds(pl.multiple_of((half * 4 + segment) * 256, 256), 256), :]
    low_lanes = lax.broadcasted_iota(jnp.int32, (256, 128), 1) < 64
    left[0:256, :] = mine
    for s in range(4):
        sl = slice(s * 128, (s + 1) * 128)
        other = pltpu.roll(mine[:, sl].astype(jnp.float32), 64, 1)
        left[256:512, sl] = jnp.where(low_lanes, other, -other).astype(jnp.bfloat16)
    dims = (((1,), (1,)), ((), ()))

    def correlate(step, carry):
        rows = pl.ds(pl.multiple_of(step * 256, 256), 256)
        gram = lax.dot_general(left[...], ordered[rows, :], dims, preferred_element_type=jnp.float32)
        gram = gram * (1.0 / NB)
        real_ref[:, rows] = gram[0:256]
        imag_ref[:, rows] = gram[256:512]
        return carry

    lax.fori_loop(0, 8, correlate, 0)

    for kind, y_from in enumerate((y, down, up, across_from)):
        arrived(plane(y_from, core), send_c.at[kind])
    for kind in range(3):
        arrived(plane(y, core), send_y.at[kind])
    arrived(spectra.at[pl.ds(0, 63 * 16), :], send_a)
    own_beam.wait()
    arrived(formed.at[pl.ds(0, 127)], send_b)
    arrived(beams_ref.at[pl.ds(0, 127)], recv_b)


def finish_kernel(
    real_ref, imag_ref, beams_ref, high_hbm, low_hbm, real_hbm, imag_hbm, series_hbm,
    high_ref, low_ref, wide, turned, series, out_sem, load,
):
    loads = [
        pltpu.make_async_copy(high_hbm, high_ref, load.at[0]),
        pltpu.make_async_copy(low_hbm, low_ref, load.at[1]),
    ]
    for copy in loads:
        copy.start()
    copies = [
        pltpu.make_async_copy(
            source.at[pl.ds(i * 64, 64)], target.at[0, 0, pl.ds(i * 64, 64)], out_sem.at[n * 4 + i]
        )
        for n, (source, target) in enumerate(((real_ref, real_hbm), (imag_ref, imag_hbm)))
        for i in range(4)
    ]
    for copy in copies:
        copy.start()
    for i in range(128):
        wide[i * 4 : (i + 1) * 4, :] = beams_ref[i].astype(jnp.float32)
    for h in range(2):
        for s in range(4):
            block = jnp.transpose(wide[pl.ds(h * 4 + s, 64, stride=8), :])
            for part in range(4):
                turned[h * 128 + s * 32 : h * 128 + (s + 1) * 32, part * 64 : (part + 1) * 64] = block[
                    part * 32 : (part + 1) * 32
                ].astype(jnp.bfloat16)
    for copy in loads:
        copy.wait()
    out = jnp.dot(turned[...], high_ref[...], preferred_element_type=jnp.float32)
    out += jnp.dot(turned[...], low_ref[...], preferred_element_type=jnp.float32)
    for h in range(2):
        for q in range(2):
            series[pl.ds(h * 256 + q, 128, stride=2), :] = out[
                h * 128 : (h + 1) * 128, q * 128 : (q + 1) * 128
            ]
    copies.append(pltpu.make_async_copy(series, series_hbm, out_sem.at[8]))
    copies[8].start()
    for copy in copies:
        copy.wait()


VMEM = pl.BlockSpec(memory_space=pltpu.VMEM)
HBM = pl.BlockSpec(memory_space=pltpu.HBM)


def in_hbm(array):
    return pltpu.with_memory_space_constraint(array, pltpu.HBM)


def per_device(voltages, slot_of_antenna, antenna_positions, beam_directions):
    high, low = forward_tables()
    real, imag, received = pl.pallas_call(
        kernel,
        out_shape=(
            jax.ShapeDtypeStruct((256, A), jnp.float32),
            jax.ShapeDtypeStruct((256, A), jnp.float32),
            jax.ShapeDtypeStruct((128, 4, 128), jnp.bfloat16),
        ),
        in_specs=[HBM] * 7,
        out_specs=(VMEM, VMEM, VMEM),
        scratch_shapes=[
            pltpu.VMEM((2, 16, 4096), jnp.bfloat16),
            pltpu.VMEM((256, 256), jnp.bfloat16),
            pltpu.VMEM((256, 256), jnp.bfloat16),
            pltpu.VMEM((16, 128), jnp.int32),
            pltpu.VMEM((2, A), jnp.int32),
            pltpu.VMEM((2, BEAMS), jnp.int32),
            pltpu.VMEM((1, 128), jnp.float32),
            pltpu.VMEM((2, 512, 128), jnp.float32),
            pltpu.VMEM((512, 256), jnp.bfloat16),
            pltpu.VMEM((1024, 128), jnp.float32),
            pltpu.VMEM((1024, 128), jnp.bfloat16),
            pltpu.VMEM((A, 512), jnp.bfloat16),
            pltpu.VMEM((A, A), jnp.bfloat16),
            pltpu.VMEM((256, A), jnp.bfloat16),
            pltpu.VMEM((256, A), jnp.bfloat16),
            pltpu.VMEM((A, 512), jnp.bfloat16),
            pltpu.VMEM((512, 512), jnp.bfloat16),
            pltpu.VMEM((512, 128), jnp.float32),
            pltpu.VMEM((128, 4, 128), jnp.bfloat16),
            pltpu.SemaphoreType.DMA,
            pltpu.SemaphoreType.DMA((16,)),
            pltpu.SemaphoreType.DMA((3,)),
            pltpu.SemaphoreType.DMA((3, 16)),
            pltpu.SemaphoreType.DMA((4,)),
            pltpu.SemaphoreType.DMA((4,)),
            pltpu.SemaphoreType.DMA,
            pltpu.SemaphoreType.DMA,
            pltpu.SemaphoreType.DMA,
            pltpu.SemaphoreType.DMA((7,)),
            pltpu.SemaphoreType.REGULAR,
            pltpu.SemaphoreType.REGULAR,
        ],
        compiler_params=pltpu.CompilerParams(
            collective_id=0, has_side_effects=True, vmem_limit_bytes=32 * 2**20
        ),
        name="correlator",
    )(
        *(
            in_hbm(array)
            for array in (
                voltages,
                jnp.asarray(high),
                jnp.asarray(low),
                slot_of_antenna.reshape(16, 128),
                antenna_positions.T,
                beam_directions.T,
                jnp.asarray(steering_table()),
            )
        )
    )
    inverse_high, inverse_low = inverse_tables()
    real, imag, series = pl.pallas_call(
        finish_kernel,
        out_shape=(
            jax.ShapeDtypeStruct((1, 1, 256, A), jnp.float32),
            jax.ShapeDtypeStruct((1, 1, 256, A), jnp.float32),
            jax.ShapeDtypeStruct((512, 128), jnp.float32),
        ),
        in_specs=[VMEM] * 3 + [HBM] * 2,
        out_specs=[HBM] * 3,
        scratch_shapes=[
            pltpu.VMEM((256, 256), jnp.bfloat16),
            pltpu.VMEM((256, 256), jnp.bfloat16),
            pltpu.VMEM((512, 128), jnp.float32),
            pltpu.VMEM((256, 256), jnp.bfloat16),
            pltpu.VMEM((512, 128), jnp.float32),
            pltpu.SemaphoreType.DMA((9,)),
            pltpu.SemaphoreType.DMA((2,)),
        ],
        compiler_params=pltpu.CompilerParams(vmem_limit_bytes=16 * 2**20),
        name="finish",
    )(
        real,
        imag,
        received,
        in_hbm(jnp.asarray(inverse_high)),
        in_hbm(jnp.asarray(inverse_low)),
    )
    series = series.reshape(2, 128, 2, 128).transpose(0, 2, 1, 3).reshape(2, 1, 1, 2, NB * 64)
    return (real, imag, series)


def solution(mesh):
    in_specs = (P(None, "band", "segment"), P(), P(), P())
    out_specs = (
        P("band", "segment", None, None),
        P("band", "segment", None, None),
        P(None, "segment", "band", None, None),
    )
    return jax.shard_map(
        per_device, mesh=mesh, in_specs=in_specs, out_specs=out_specs, check_vma=False
    )
```
